256 devices in a mesh: pipe: 16 (over z, core), tensor: 16 (over y, x).
Axes of the slice: x: 4, y: 4, z: 8, core: 2. Of those that a mesh axis runs over, the one named last changes fastest.
Arguments:
- section_inputs: bfloat16 [16, 8, 128, 12288], P('pipe', None, None, 'tensor'), may hold values from -6 to 6
- out_grad: bfloat16 [8, 128, 12288], P(None, None, 'tensor'), may hold values from -6 to 6
- w_first: bfloat16 [16, 1, 96, 128, 128], P('pipe', None, 'tensor'), may hold values from -0.5 to 0.5
- w_second: bfloat16 [16, 1, 96, 128, 128], P('pipe', None, 'tensor'), may hold values from -0.5 to 0.5
- drop_flags: int32 [16, 1], P('pipe'), may hold values 0 or 1
- perm: int32 [16, 1, 12288], P('pipe'), may hold values from 0 to 12287, as said below
Outputs:
- input_grads: bfloat16 [16, 8, 128, 12288], P('pipe', None, None, 'tensor')
- grad_first: float32 [16, 1, 96, 128, 128], P('pipe', None, 'tensor')
- grad_second: float32 [16, 1, 96, 128, 128], P('pipe', None, 'tensor')
The draws below stay inside these ranges and needn't reach their ends.
Inputs may be any that keep to these rules, and one draw needn't show every extreme that they name: For each section and layer, perm is a permutation of 0 to 12287, and for every two block groups g and h exactly 48 of the positions h * 768 to (h + 1) * 768 - 1 hold a feature of group g, that is a number from g * 768 to (g + 1) * 768 - 1.
All inputs are finite; a program needn't handle non-finite values. No bound on the sum of `drop_flags` on one device may be relied on, other than what follows from the above.
Results may differ from the reference program's by a relative error of at most 0.023.
Values may be sent and summed in bfloat16 or wider, within the bound.
No kernel may reach another device: no remote copies, remote signals or barrier semaphores. Data moves between devices by JAX's collectives and lax.ppermute only.
A program may use at most 128 MiB of HBM per device.

```python
import jax
import jax.numpy as jnp

NB = 96
BS = 128
W = 12288
TOK = 128
MB = 8
LAYERS = 1
SECTIONS = 16
GROUPS = 16


def draw_perm(key, part):
    feat_count = W // GROUPS
    per_peer = feat_count // GROUPS

    def one_layer(layer_key):
        first_key, second_key = jax.random.split(layer_key)
        spread = jax.vmap(lambda k: jax.random.permutation(k, feat_count))(jax.random.split(first_key, GROUPS))
        starts = jnp.arange(GROUPS, dtype=jnp.int32)[:, None] * feat_count
        sources = (starts + spread.astype(jnp.int32)).reshape(GROUPS, GROUPS, per_peer)
        arrived = jnp.transpose(sources, (1, 0, 2)).reshape(GROUPS, feat_count)
        placed = jax.vmap(lambda k: jax.random.permutation(k, feat_count))(jax.random.split(second_key, GROUPS))
        inverse_place = jnp.argsort(placed, axis=1)
        return jnp.take_along_axis(arrived, inverse_place, axis=1).reshape(W)
    keys = jax.random.split(key, SECTIONS * LAYERS)
    return jax.vmap(one_layer)(keys).reshape(SECTIONS, LAYERS, W).astype(jnp.int32)


def set_ends(entries, own_key, least, largest):
    index_at = [jax.random.randint(jax.random.fold_in(own_key, axis), (), 0, length) for axis, length in enumerate(entries.shape)]
    longest = entries.shape.index(max(entries.shape))
    beside = index_at[:longest] + [(index_at[longest] + 1) % entries.shape[longest]] + index_at[longest + 1:]
    return entries.at[tuple(index_at)].set(least).at[tuple(beside)].set(largest)


def steps_of(key, extent, cuts, least, high):
    level, own = 1.0, jax.random.fold_in(key, 6)
    for position, blocks in cuts:
        heights = jnp.exp(jax.random.uniform(jax.random.fold_in(own, position), (blocks,), jnp.float32, least / len(cuts), high / len(cuts)))
        level = level * jnp.repeat(heights, extent[position] // blocks).reshape([-1 if axis == position else 1 for axis in range(len(extent))])
    return level


def centred(rng, extent, deviation, most, pieces=(), kind=jnp.bfloat16):
    loudness = steps_of(rng, extent, pieces, -0.22, 0.18) if pieces else 1.0
    entries = jax.random.normal(rng, extent, jnp.float32) * deviation * loudness
    return jnp.minimum(jnp.maximum(entries, -most), most).astype(kind)


def setup_inputs(seed: int = 0) -> dict:
    arg_keys = jax.random.split(jax.random.key(seed), 7)
    return {
        "section_inputs": centred(arg_keys[0], (SECTIONS, MB, TOK, W), 1.0, 6.0, ((0, 16), (3, 16))),
        "out_grad": centred(arg_keys[1], (MB, TOK, W), 1.0, 6.0, ((2, 16),)),
        "w_first": centred(arg_keys[2], (SECTIONS, LAYERS, NB, BS, BS), BS ** -0.5, 0.5, ((0, 16), (2, 16))),
        "w_second": centred(arg_keys[3], (SECTIONS, LAYERS, NB, BS, BS), BS ** -0.5, 0.5, ((0, 16), (2, 16))),
        "drop_flags": set_ends((jax.random.randint(arg_keys[4], (SECTIONS, LAYERS), 0, 4) < 3).astype(jnp.int32), jax.random.fold_in(arg_keys[4], 1), 0, 1),
        "perm": draw_perm(jax.random.fold_in(arg_keys[6], 71), 0),
    }


gelu_scale = 0.7978845608028654
gelu_cubic = 0.044715


def gelu_value(values):
    inner = gelu_scale * (values + gelu_cubic * values * values * values)
    return 0.5 * values * (1.0 + jnp.tanh(inner))


def gelu_slope(values):
    tangent = jnp.tanh(gelu_scale * (values + gelu_cubic * values * values * values))
    return 0.5 * (1.0 + tangent) + 0.5 * values * (1.0 - tangent * tangent) * gelu_scale * (1.0 + 3.0 * gelu_cubic * values * values)


def blocked(values):
    return values.reshape(values.shape[:-1] + (NB, BS)).astype(jnp.float32)


def block_product(values, weight):
    result = jnp.einsum('mtbi,bij->mtbj', blocked(values), weight.astype(jnp.float32))
    return result.reshape(values.shape)


def block_back(values, weight):
    result = jnp.einsum('mtbj,bij->mtbi', blocked(values), weight.astype(jnp.float32))
    return result.reshape(values.shape)


def block_outer(left, right):
    return jnp.einsum('mtbi,mtbj->bij', blocked(left), blocked(right))


def reference(section_inputs, out_grad, w_first, w_second, drop_flags, perm):
    cotangent = out_grad
    grads_in = []
    grads_first = []
    grads_second = []
    for section_index in range(SECTIONS - 1, -1, -1):
        layer_inputs = [section_inputs[section_index]]
        saved_pairs = []
        for layer_index in range(LAYERS):
            current = layer_inputs[-1]
            keep_factor = drop_flags[section_index, layer_index].astype(jnp.float32)
            before = block_product(current, w_first[section_index, layer_index])
            hidden = gelu_value(before).astype(jnp.bfloat16)
            mixed = jnp.take(hidden, perm[section_index, layer_index], axis=2)
            branch = block_product(mixed, w_second[section_index, layer_index])
            layer_inputs.append((current.astype(jnp.float32) + keep_factor * branch).astype(jnp.bfloat16))
            saved_pairs.append((before, mixed))
        grad_now = cotangent
        first_list = []
        second_list = []
        for layer_index in range(LAYERS - 1, -1, -1):
            current = layer_inputs[layer_index]
            before, mixed = saved_pairs[layer_index]
            keep_factor = drop_flags[section_index, layer_index].astype(jnp.float32)
            grad_branch = (keep_factor * grad_now.astype(jnp.float32)).astype(jnp.bfloat16)
            second_list.append(block_outer(mixed, grad_branch))
            grad_mixed = block_back(grad_branch, w_second[section_index, layer_index]).astype(jnp.bfloat16)
            inverse = jnp.argsort(perm[section_index, layer_index]).astype(jnp.int32)
            grad_hidden = jnp.take(grad_mixed, inverse, axis=2)
            grad_before = (grad_hidden.astype(jnp.float32) * gelu_slope(before)).astype(jnp.bfloat16)
            first_list.append(block_outer(current, grad_before))
            grad_now = (grad_now.astype(jnp.float32) + block_back(grad_before, w_first[section_index, layer_index])).astype(jnp.bfloat16)
        cotangent = grad_now
        grads_in.append(grad_now)
        grads_first.append(jnp.stack(first_list[::-1]))
        grads_second.append(jnp.stack(second_list[::-1]))
    return (jnp.stack(grads_in[::-1]), jnp.stack(grads_first[::-1]), jnp.stack(grads_second[::-1]))
```

```python
import functools

import jax
import jax.numpy as jnp
from jax import lax
from jax.experimental import pallas as pl
from jax.experimental.pallas import tpu as pltpu
from jax.sharding import PartitionSpec as P

gelu_scale = 0.7978845608028654
gelu_cubic = 0.044715
bf16 = jnp.bfloat16
f32 = jnp.float32


def dot(left, right, dims):
    return lax.dot_general(left, right, (dims, ((), ())), preferred_element_type=f32)


NN = ((1,), (0,))
NT = ((1,), (1,))
TN = ((0,), (0,))


def whole(space=pltpu.VMEM):
    return pl.BlockSpec(memory_space=space)


def prep_kernel(group_ref, drop_ref, perm_ref, w1_ref, w2_ref, w1d_ref, w2d_ref, pick_first_ref, pick_second_ref):
    groups, feats = perm_ref.shape
    blocks, size, _ = w1_ref.shape
    per_peer = feats // groups
    own_group = group_ref[0]
    keep = drop_ref[0].astype(f32)
    base = own_group * feats
    rows = lax.broadcasted_iota(jnp.int32, (feats, feats), 0)
    cols = lax.broadcasted_iota(jnp.int32, (feats, feats), 1)
    before = jnp.where(rows < cols, 1.0, 0.0).astype(bf16)
    perm = perm_ref[...]
    mine = (perm >= base) & (perm < base + feats)
    rank = dot(jnp.where(mine, 1.0, 0.0).astype(bf16), before, NN)
    rank = jnp.where(mine, rank, -1.0).astype(jnp.int32)
    local = (perm - base).astype(f32)
    counter = lax.broadcasted_iota(jnp.int32, (per_peer, feats), 0)
    lane = lax.broadcasted_iota(jnp.int32, (per_peer, feats), 1)
    for peer in range(groups):
        hit = counter == rank[peer : peer + 1, :]
        source = jnp.sum(jnp.where(hit, local[peer : peer + 1, :], 0.0), axis=1, keepdims=True)
        pick_first_ref[peer * per_peer : (peer + 1) * per_peer, :] = jnp.where(
            lane == source.astype(jnp.int32), 1.0, 0.0
        ).astype(bf16)
    own = perm_ref[pl.ds(own_group, 1), :]
    start = lax.broadcasted_iota(jnp.int32, (groups, feats), 0)
    from_group = (own >= start * feats) & (own < start * feats + feats)
    marks = jnp.where(from_group, 1.0, 0.0)
    place = dot(marks.astype(bf16), before, NN) + start.astype(f32) * per_peer
    slot = jnp.sum(marks * place, axis=0, keepdims=True).astype(jnp.int32)
    arrive = jnp.where(rows == slot, 1.0, 0.0)
    arrive_bf = arrive.astype(bf16)
    pick_second_ref[...] = jnp.transpose(arrive).astype(bf16)
    for block in range(blocks):
        span = slice(block * size, (block + 1) * size)
        w1d_ref[:, span] = dot(pick_first_ref[:, span], w1_ref[block], NT).astype(bf16)
        w2d_ref[:, span] = (keep * dot(arrive_bf[:, span], w2_ref[block], NN)).astype(bf16)


def forward_kernel(x_ref, w1d_ref, hidden_ref, slope_ref):
    groups, _, per_peer, tokens = hidden_ref.shape
    v = dot(w1d_ref[...], x_ref[0], NT)
    u = jnp.tanh(gelu_scale * (v + gelu_cubic * v * v * v))
    hidden = (0.5 * v * (1.0 + u)).astype(bf16)
    hidden_ref[...] = hidden.reshape(groups, 1, per_peer, tokens)
    slope_ref[0] = 0.5 * (1.0 + u) + 0.5 * v * (1.0 - u * u) * gelu_scale * (1.0 + 3.0 * gelu_cubic * v * v)


def send_kernel(step_ref, where_ref, incoming_ref, out_grad_ref, w2d_ref, gin_old, gin_ref, mixed_ref):
    del gin_old
    last = where_ref[1] == 1
    g = jnp.where(last, out_grad_ref[0], incoming_ref[...])
    gin_ref[0] = g
    groups, per_peer, tokens = mixed_ref.shape
    mixed_ref[...] = dot(w2d_ref[...], g, NT).astype(bf16).reshape(groups, per_peer, tokens)


def receive_kernel(step_ref, where_ref, returned_ref, slope_ref, w1d_ref, gin_ref, da_old, gout_old, da_ref, gout_ref, g_ref):
    del da_old, gout_old
    groups, per_peer, tokens = returned_ref.shape
    dh = returned_ref[...].reshape(groups * per_peer, tokens).astype(f32)
    da = jnp.transpose(dh * slope_ref[0]).astype(bf16)
    da_ref[0] = da
    g = (gin_ref[0].astype(f32) + dot(da, w1d_ref[...], NN)).astype(bf16)
    gout_ref[0] = g
    g_ref[...] = g


def grad_kernel(start_ref, drop_ref, x_ref, da_ref, z_ref, gin_ref, gout_ref, pick_first_ref, pick_second_ref, grads_ref, first_ref, second_ref):
    micro = pl.program_id(0)
    blocks, size, _ = first_ref.shape
    keep = drop_ref[0].astype(f32)
    grads_ref[0] = gout_ref[0]
    da = dot(da_ref[0], pick_first_ref[...], NN).astype(bf16)
    groups, _, per_peer, tokens = z_ref.shape
    z = dot(pick_second_ref[...], z_ref[...].reshape(groups * per_peer, tokens), NN).astype(bf16)
    x = x_ref[0]
    g = gin_ref[0]

    @pl.when(micro == 0)
    def _():
        first_ref[...] = jnp.zeros_like(first_ref)
        second_ref[...] = jnp.zeros_like(second_ref)

    for block in range(blocks):
        span = slice(block * size, (block + 1) * size)
        first_ref[block] += dot(x[:, span], da[:, span], TN)
        second_ref[block] += keep * dot(z[span, :], g[:, span], NN)


def on_device(section_inputs, out_grad, w_first, w_second, drop_flags, perm):
    sections = lax.axis_size("pipe")
    section = lax.axis_index("pipe").astype(jnp.int32)
    groups = lax.axis_size("tensor")
    group = lax.axis_index("tensor").astype(jnp.int32)
    x = section_inputs[0]
    micros, tokens, feats = x.shape
    blocks, size = w_first.shape[2], w_first.shape[3]
    per_peer = feats // groups
    steps = micros + sections - 1
    drop = drop_flags.reshape(1)
    sds = jax.ShapeDtypeStruct
    params = pltpu.CompilerParams(vmem_limit_bytes=24 * 1024 * 1024)

    w1d, w2d, pick_first, pick_second = pl.pallas_call(
        prep_kernel,
        in_specs=[whole(pltpu.SMEM), whole(pltpu.SMEM), whole(), whole(), whole()],
        out_specs=[whole()] * 4,
        out_shape=[sds((feats, feats), bf16)] * 4,
        compiler_params=params,
        name="prep",
    )(group.reshape(1), drop, perm.reshape(groups, feats), w_first[0, 0], w_second[0, 0])

    hidden, slope = pl.pallas_call(
        forward_kernel,
        grid=(micros,),
        in_specs=[
            pl.BlockSpec((1, tokens, feats), lambda m: (m, 0, 0)),
            pl.BlockSpec((feats, feats), lambda m: (0, 0)),
        ],
        out_specs=[
            pl.BlockSpec((groups, 1, per_peer, tokens), lambda m: (0, m, 0, 0)),
            pl.BlockSpec((1, feats, tokens), lambda m: (m, 0, 0)),
        ],
        out_shape=[sds((groups, micros, per_peer, tokens), bf16), sds((micros, feats, tokens), f32)],
        compiler_params=params,
        name="forward",
    )(x, w1d)
    z = lax.all_to_all(hidden, "tensor", 0, 0, tiled=True)

    where = jnp.stack([sections - 1 - section, (section == sections - 1).astype(jnp.int32)])

    def pick(k, w):
        return jnp.clip(k[0] - w[0], 0, micros - 1)

    send = pl.pallas_call(
        send_kernel,
        grid_spec=pltpu.PrefetchScalarGridSpec(
            num_scalar_prefetch=2,
            grid=(1,),
            in_specs=[
                pl.BlockSpec((tokens, feats), lambda i, k, w: (0, 0)),
                pl.BlockSpec((1, tokens, feats), lambda i, k, w: (pick(k, w), 0, 0)),
                pl.BlockSpec((feats, feats), lambda i, k, w: (0, 0)),
                whole(pl.ANY),
            ],
            out_specs=[
                pl.BlockSpec((1, tokens, feats), lambda i, k, w: (k[0], 0, 0)),
                pl.BlockSpec((groups, per_peer, tokens), lambda i, k, w: (0, 0, 0)),
            ],
        ),
        out_shape=[sds((steps, tokens, feats), bf16), sds((groups, per_peer, tokens), bf16)],
        input_output_aliases={5: 0},
        compiler_params=params,
        name="send",
    )
    receive = pl.pallas_call(
        receive_kernel,
        grid_spec=pltpu.PrefetchScalarGridSpec(
            num_scalar_prefetch=2,
            grid=(1,),
            in_specs=[
                pl.BlockSpec((groups, per_peer, tokens), lambda i, k, w: (0, 0, 0)),
                pl.BlockSpec((1, feats, tokens), lambda i, k, w: (pick(k, w), 0, 0)),
                pl.BlockSpec((feats, feats), lambda i, k, w: (0, 0)),
                pl.BlockSpec((1, tokens, feats), lambda i, k, w: (k[0], 0, 0)),
                whole(pl.ANY),
                whole(pl.ANY),
            ],
            out_specs=[
                pl.BlockSpec((1, tokens, feats), lambda i, k, w: (k[0], 0, 0)),
                pl.BlockSpec((1, tokens, feats), lambda i, k, w: (k[0], 0, 0)),
                pl.BlockSpec((tokens, feats), lambda i, k, w: (0, 0)),
            ],
        ),
        out_shape=[sds((steps, tokens, feats), bf16)] * 2 + [sds((tokens, feats), bf16)],
        input_output_aliases={6: 0, 7: 1},
        compiler_params=params,
        name="receive",
    )
    route = [(i, i - 1) for i in range(1, sections)]

    def advance(k, carry):
        g, gin, da, gout = carry
        at = jnp.full((1,), k, jnp.int32)
        incoming = lax.ppermute(g, "pipe", route)
        gin, outgoing = send(at, where, incoming, out_grad, w2d, gin)
        returned = lax.all_to_all(outgoing, "tensor", 0, 0, tiled=True)
        da, gout, g = receive(at, where, returned, slope, w1d, gin, da, gout)
        return (g, gin, da, gout)

    def blank():
        return jnp.zeros((steps, tokens, feats), bf16)

    _, gin, da, gout = lax.fori_loop(
        0, steps, advance, (jnp.zeros((tokens, feats), bf16), blank(), blank(), blank())
    )

    grads, first, second = pl.pallas_call(
        grad_kernel,
        grid_spec=pltpu.PrefetchScalarGridSpec(
            num_scalar_prefetch=2,
            grid=(micros,),
            in_specs=[
                pl.BlockSpec((1, tokens, feats), lambda m, w, d: (m, 0, 0)),
                pl.BlockSpec((1, tokens, feats), lambda m, w, d: (w[0] + m, 0, 0)),
                pl.BlockSpec((groups, 1, per_peer, tokens), lambda m, w, d: (0, m, 0, 0)),
                pl.BlockSpec((1, tokens, feats), lambda m, w, d: (w[0] + m, 0, 0)),
                pl.BlockSpec((1, tokens, feats), lambda m, w, d: (w[0] + m, 0, 0)),
                pl.BlockSpec((feats, feats), lambda m, w, d: (0, 0)),
                pl.BlockSpec((feats, feats), lambda m, w, d: (0, 0)),
            ],
            out_specs=[
                pl.BlockSpec((1, tokens, feats), lambda m, w, d: (m, 0, 0)),
                pl.BlockSpec((blocks, size, size), lambda m, w, d: (0, 0, 0)),
                pl.BlockSpec((blocks, size, size), lambda m, w, d: (0, 0, 0)),
            ],
        ),
        out_shape=[
            sds((micros, tokens, feats), bf16),
            sds((blocks, size, size), f32),
            sds((blocks, size, size), f32),
        ],
        compiler_params=params,
        name="grads",
    )(where, drop, x, da, z, gin, gout, pick_first, pick_second)
    return (grads[None], first[None, None], second[None, None])


def solution(mesh):
    placed = (
        P("pipe", None, None, "tensor"),
        P(None, None, "tensor"),
        P("pipe", None, "tensor", None, None),
        P("pipe", None, "tensor", None, None),
        P("pipe", None),
        P("pipe", None, None),
    )
    return jax.shard_map(
        on_device,
        mesh=mesh,
        in_specs=placed,
        out_specs=(
            P("pipe", None, None, "tensor"),
            P("pipe", None, "tensor", None, None),
            P("pipe", None, "tensor", None, None),
        ),
        check_vma=False,
    )
```

```python
import jax
import jax.numpy as jnp
from jax import lax
from jax.experimental import pallas as pl
from jax.experimental.pallas import tpu as pltpu
from jax.sharding import PartitionSpec as P

MEMBERS = 2
CHUNKS = 2

gelu_scale = 0.7978845608028654
gelu_cubic = 0.044715
bf16 = jnp.bfloat16
f32 = jnp.float32
i32 = jnp.int32
sds = jax.ShapeDtypeStruct

NN = ((1,), (0,))
NT = ((1,), (1,))
LANES = 128


def dot(left, right, dims):
    return lax.dot_general(left, right, (dims, ((), ())), preferred_element_type=f32)


def whole(space=pltpu.VMEM):
    return pl.BlockSpec(memory_space=space)


def prep_kernel(group_ref, drop_ref, perm_ref, w1_ref, w2_ref, packed_ref, first_ref, second_ref):
    groups, feats = perm_ref.shape
    blocks, size, _ = w1_ref.shape
    per_peer = feats // groups
    own_group = group_ref[0]
    keep = drop_ref[0].astype(f32)
    base = own_group * feats
    rows = lax.broadcasted_iota(i32, (feats, feats), 0)
    cols = lax.broadcasted_iota(i32, (feats, feats), 1)
    before = jnp.where(rows < cols, 1.0, 0.0).astype(bf16)
    perm = perm_ref[...]
    mine = (perm >= base) & (perm < base + feats)
    rank = dot(jnp.where(mine, 1.0, 0.0).astype(bf16), before, NN)
    rank = jnp.where(mine, rank, -1.0).astype(i32)
    local = (perm - base).astype(f32)
    counter = lax.broadcasted_iota(i32, (per_peer, feats), 0)
    lane = lax.broadcasted_iota(i32, (per_peer, feats), 1)
    parts = []
    for peer in range(groups):
        hit = counter == rank[peer : peer + 1, :]
        source = jnp.sum(jnp.where(hit, local[peer : peer + 1, :], 0.0), axis=1, keepdims=True)
        parts.append(jnp.where(lane == source.astype(i32), 1.0, 0.0))
    leave = jnp.concatenate(parts, axis=0)
    own = perm_ref[pl.ds(own_group, 1), :]
    start = lax.broadcasted_iota(i32, (groups, feats), 0)
    from_group = (own >= start * feats) & (own < start * feats + feats)
    marks = jnp.where(from_group, 1.0, 0.0)
    place = dot(marks.astype(bf16), before, NN) + start.astype(f32) * per_peer
    slot = jnp.sum(marks * place, axis=0, keepdims=True).astype(i32)
    arrive = jnp.where(rows == slot, 1.0, 0.0)
    first_ref[...] = jnp.transpose(leave).astype(bf16)
    second_ref[...] = jnp.transpose(arrive).astype(bf16)
    leave = leave.astype(bf16)
    arrive = arrive.astype(bf16)
    part1 = jnp.zeros((feats, size), f32)
    part2 = jnp.zeros((feats, size), f32)
    for block in range(blocks):
        span = slice(block * size, (block + 1) * size)
        part1 += dot(leave[:, span], w1_ref[block], NT)
        part2 += dot(arrive[:, span], w2_ref[block], NN)
    owner = lax.broadcasted_iota(i32, (feats, LANES), 0) // size
    column = lax.broadcasted_iota(i32, (feats, LANES), 1)
    where1 = jnp.where(column == owner, 1.0, 0.0).astype(bf16)
    where2 = jnp.where(column == owner + 8, 1.0, 0.0).astype(bf16)
    packed_ref[:, 0:size] = part1.astype(bf16)
    packed_ref[:, size : 2 * size] = (keep * part2).astype(bf16)
    packed_ref[:, 2 * size :] = (dot(leave, where1, NN) + dot(arrive, where2, NN)).astype(bf16)


def forward_kernel(x_ref, packed_ref, hidden_ref, slope_ref, *dense_refs):
    groups, _, per_peer, tokens = hidden_ref.shape
    section = pl.program_id(0)
    members = len(dense_refs) // 2
    feats = packed_ref.shape[1]
    blocks = feats // LANES
    packed = packed_ref[0].astype(f32)
    w1 = packed[:, :LANES]
    w2 = packed[:, LANES : 2 * LANES]
    dense1 = jnp.concatenate([w1 * packed[:, 2 * LANES + b : 2 * LANES + b + 1] for b in range(blocks)], axis=1)
    dense2 = jnp.concatenate([w2 * packed[:, 2 * LANES + 8 + b : 2 * LANES + 9 + b] for b in range(blocks)], axis=1)
    dense1 = dense1.astype(bf16)
    dense2 = dense2.astype(bf16)
    for member in range(members):

        @pl.when(section == member)
        def _():
            dense_refs[member][...] = dense1
            dense_refs[members + member][...] = dense2

    v = dot(dense1, x_ref[0], NT)
    u = jnp.tanh(gelu_scale * (v + gelu_cubic * v * v * v))
    hidden_ref[...] = (0.5 * v * (1.0 + u)).astype(bf16).reshape(groups, 1, per_peer, tokens)
    slope_ref[0] = 0.5 * (1.0 + u) + 0.5 * v * (1.0 - u * u) * gelu_scale * (1.0 + 3.0 * gelu_cubic * v * v)


def mix(w2_ref, g, mixed_ref):
    mixed_ref[...] = dot(w2_ref[...], g, NT).astype(bf16).reshape(mixed_ref.shape)


def head_kernel(step_ref, where_ref, incoming_ref, out_grad_ref, w2_ref, old_ref, stored_ref, g_ref, mixed_ref):
    del old_ref
    g = jnp.where(where_ref[1] == 1, out_grad_ref[0], incoming_ref[...])
    stored_ref[0, 0] = g
    g_ref[...] = g
    mix(w2_ref, g, mixed_ref)


def back_kernel(has_next, *refs):
    step_ref, where_ref, returned_ref, g_in_ref, slope_ref, w1_ref = refs[:6]
    refs = refs[6:]
    if has_next:
        w2_ref, refs = refs[0], refs[1:]
    _, _, da_ref, stored_ref, g_ref = refs[:5]
    groups, per_peer, tokens = returned_ref.shape
    dh = returned_ref[...].reshape(groups * per_peer, tokens).astype(f32)
    da = dh * slope_ref[0]
    da_ref[0, 0] = da.astype(bf16)
    g = g_in_ref[...].astype(f32) + dot(jnp.transpose(da).astype(bf16), w1_ref[...], NN)
    g = g.astype(bf16)
    stored_ref[0, 0] = g
    g_ref[...] = g
    if has_next:
        mix(w2_ref, g, refs[5])


def partial_kernel(where_ref, da_ref, cot_ref, out_ref, x_ref, z_ref, mask_ref, first_ref, second_ref, grads_ref):
    feats = da_ref.shape[2]
    blocks = feats // LANES
    groups, _, per_peer, tokens = z_ref.shape
    grads_ref[0] = out_ref[0, 0]
    mask = mask_ref[0].astype(f32)
    one = dot(da_ref[0, 0], x_ref[0], NN)
    two = dot(z_ref[...].reshape(groups * per_peer, tokens), cot_ref[0, 0], NN)
    one = sum(one[:, b * LANES : (b + 1) * LANES] * mask[:, b : b + 1] for b in range(blocks))
    two = sum(two[:, b * LANES : (b + 1) * LANES] * mask[:, 8 + b : 9 + b] for b in range(blocks))

    @pl.when(pl.program_id(1) == 0)
    def _():
        first_ref[0] = one
        second_ref[0] = two

    @pl.when(pl.program_id(1) != 0)
    def _():
        first_ref[0] += one
        second_ref[0] += two


def unpick(pick, values):
    high = values.astype(bf16)
    rest = values - high.astype(f32)
    middle = rest.astype(bf16)
    low = (rest - middle.astype(f32)).astype(bf16)
    return dot(pick, high, NN) + dot(pick, middle, NN) + dot(pick, low, NN)


def final_kernel(drop_ref, one_ref, two_ref, pick1_ref, pick2_ref, first_ref, second_ref):
    blocks, size, _ = first_ref.shape
    keep = drop_ref[0].astype(f32)
    one = unpick(pick1_ref[...], jnp.sum(one_ref[...], axis=0))
    two = keep * unpick(pick2_ref[...], jnp.sum(two_ref[...], axis=0))
    for block in range(blocks):
        span = slice(block * size, (block + 1) * size)
        first_ref[block] = jnp.transpose(one[span, :])
        second_ref[block] = two[span, :]


def on_device(section_inputs, out_grad, w_first, w_second, drop_flags, perm):
    J, M = MEMBERS, CHUNKS
    rows = lax.axis_size("pipe")
    row = lax.axis_index("pipe").astype(i32)
    stages = rows // J
    stage, member = row // J, row % J
    groups = lax.axis_size("tensor")
    group = lax.axis_index("tensor").astype(i32)
    micros, micro_tokens, feats = section_inputs.shape[1:]
    total = micros * micro_tokens
    n = total // J
    c = n // M
    blocks, size = w_first.shape[2], w_first.shape[3]
    per_peer = feats // groups
    steps = M + stages - 1
    drop = drop_flags.reshape(1)
    params = pltpu.CompilerParams(vmem_limit_bytes=58 * 1024 * 1024)
    index_groups = [[s * J + j for j in range(J)] for s in range(stages)]

    def by_source(mine, other):
        return jnp.stack([jnp.where(member == 0, mine, other), jnp.where(member == 0, other, mine)])

    def partner(value):
        return lax.ppermute(value, "pipe", [(i, i ^ 1) for i in range(rows)])

    def exchange(value):
        if J == 2:
            mine = lax.dynamic_index_in_dim(value, member, 0, keepdims=False)
            other = lax.dynamic_index_in_dim(value, 1 - member, 0, keepdims=False)
            return by_source(mine, partner(other))
        return lax.all_to_all(value, "pipe", 0, 0, tiled=True, axis_index_groups=index_groups)

    def collect(value):
        if J == 2:
            return by_source(value, partner(value))
        return lax.all_gather(value, "pipe", axis_index_groups=index_groups)

    xs = exchange(section_inputs.reshape(J, n, feats))
    packed, pick1, pick2 = pl.pallas_call(
        prep_kernel,
        in_specs=[whole(pltpu.SMEM), whole(pltpu.SMEM), whole(), whole(), whole()],
        out_specs=[whole()] * 3,
        out_shape=[sds((feats, 3 * LANES), bf16)] + [sds((feats, feats), bf16)] * 2,
        compiler_params=params,
        name="prep",
    )(group.reshape(1), drop, perm.reshape(groups, feats), w_first[0, 0], w_second[0, 0])
    packed = collect(packed)

    outs = pl.pallas_call(
        forward_kernel,
        grid=(J,),
        in_specs=[
            pl.BlockSpec((1, n, feats), lambda j: (j, 0, 0)),
            pl.BlockSpec((1, feats, 3 * LANES), lambda j: (j, 0, 0)),
        ],
        out_specs=[
            pl.BlockSpec((groups, 1, per_peer, n), lambda j: (0, j, 0, 0)),
            pl.BlockSpec((1, feats, n), lambda j: (j, 0, 0)),
        ]
        + [pl.BlockSpec((feats, feats), lambda j: (0, 0))] * (2 * J),
        out_shape=[sds((groups, J, per_peer, n), bf16), sds((J, feats, n), f32)]
        + [sds((feats, feats), bf16)] * (2 * J),
        compiler_params=params,
        name="forward",
    )(xs, packed)
    hidden, slope = outs[:2]
    dense1, dense2 = outs[2 : 2 + J], outs[2 + J :]
    z = lax.all_to_all(hidden, "tensor", 0, 0, tiled=True)

    where = jnp.stack([stages - 1 - stage, (stage == stages - 1).astype(i32), member * M])
    chunks = out_grad.reshape(J * M, c, feats)

    def pick(k, w):
        return jnp.clip(k[0] - w[0], 0, M - 1)

    value_spec = pl.BlockSpec((c, feats), lambda i, k, w: (0, 0))
    mixed_spec = pl.BlockSpec((groups, per_peer, c), lambda i, k, w: (0, 0, 0))
    stored_shape = sds((steps, J + 1, c, feats), bf16)
    da_shape = sds((steps, J, feats, c), bf16)
    value_shape = sds((c, feats), bf16)
    mixed_shape = sds((groups, per_peer, c), bf16)

    def stored_spec(j):
        return pl.BlockSpec((1, 1, c, feats), lambda i, k, w: (k[0], j, 0, 0))

    head = pl.pallas_call(
        head_kernel,
        grid_spec=pltpu.PrefetchScalarGridSpec(
            num_scalar_prefetch=2,
            grid=(1,),
            in_specs=[
                value_spec,
                pl.BlockSpec((1, c, feats), lambda i, k, w: (w[2] + pick(k, w), 0, 0)),
                whole(),
                whole(pl.ANY),
            ],
            out_specs=[stored_spec(J), value_spec, mixed_spec],
        ),
        out_shape=[stored_shape, value_shape, mixed_shape],
        input_output_aliases={5: 0},
        compiler_params=params,
        name="head",
    )

    def back(j):
        has_next = j > 0
        extra = 1 if has_next else 0

        def body(*refs):
            back_kernel(has_next, *refs)

        return pl.pallas_call(
            body,
            grid_spec=pltpu.PrefetchScalarGridSpec(
                num_scalar_prefetch=2,
                grid=(1,),
                in_specs=[
                    mixed_spec,
                    value_spec,
                    pl.BlockSpec((1, feats, c), lambda i, k, w: (j, 0, pick(k, w))),
                    whole(),
                ]
                + [whole()] * extra
                + [whole(pl.ANY)] * 2,
                out_specs=[
                    pl.BlockSpec((1, 1, feats, c), lambda i, k, w: (k[0], j, 0, 0)),
                    stored_spec(j),
                    value_spec,
                ]
                + [mixed_spec] * extra,
            ),
            out_shape=[da_shape, stored_shape, value_shape] + [mixed_shape] * extra,
            input_output_aliases={6 + extra: 0, 7 + extra: 1},
            compiler_params=params,
            name="back",
        )

    backs = [back(j) for j in range(J)]
    route = [(i, i - J) for i in range(J, rows)]

    def advance(k, carry):
        g, stored, da = carry
        at = jnp.full((1,), k, i32)
        if stages > 1:
            g = lax.ppermute(g, "pipe", route)
        stored, g, mixed = head(at, where, g, chunks, dense2[J - 1], stored)
        for j in reversed(range(J)):
            returned = lax.all_to_all(mixed, "tensor", 0, 0, tiled=True)
            if j > 0:
                da, stored, g, mixed = backs[j](at, where, returned, g, slope, dense1[j], dense2[j - 1], da, stored)
            else:
                da, stored, g = backs[j](at, where, returned, g, slope, dense1[j], da, stored)
        return (g, stored, da)

    carry = (
        jnp.zeros((c, feats), bf16),
        jnp.zeros(stored_shape.shape, bf16),
        jnp.zeros(da_shape.shape, bf16),
    )
    _, stored, da = lax.fori_loop(0, steps, advance, carry)

    one, two, grads = pl.pallas_call(
        partial_kernel,
        grid_spec=pltpu.PrefetchScalarGridSpec(
            num_scalar_prefetch=1,
            grid=(J, M),
            in_specs=[
                pl.BlockSpec((1, 1, feats, c), lambda j, m, w: (w[0] + m, j, 0, 0)),
                pl.BlockSpec((1, 1, c, feats), lambda j, m, w: (w[0] + m, j + 1, 0, 0)),
                pl.BlockSpec((1, 1, c, feats), lambda j, m, w: (w[0] + m, j, 0, 0)),
                pl.BlockSpec((1, c, feats), lambda j, m, w: (j, m, 0)),
                pl.BlockSpec((groups, 1, per_peer, c), lambda j, m, w: (0, j, 0, m)),
                pl.BlockSpec((1, feats, LANES), lambda j, m, w: (j, 0, 2)),
            ],
            out_specs=[
                pl.BlockSpec((1, feats, LANES), lambda j, m, w: (j, 0, 0)),
                pl.BlockSpec((1, feats, LANES), lambda j, m, w: (j, 0, 0)),
                pl.BlockSpec((1, c, feats), lambda j, m, w: (j, m, 0)),
            ],
        ),
        out_shape=[sds((J, feats, LANES), f32), sds((J, feats, LANES), f32), sds((J, n, feats), bf16)],
        compiler_params=params,
        name="partial",
    )(where, da, stored, stored, xs, z, packed)

    grads = exchange(grads)
    one = exchange(one)
    two = exchange(two)
    first, second = pl.pallas_call(
        final_kernel,
        in_specs=[whole(pltpu.SMEM)] + [whole()] * 4,
        out_specs=[whole()] * 2,
        out_shape=[sds((blocks, size, size), f32)] * 2,
        compiler_params=params,
        name="final",
    )(drop, one, two, pick1, pick2)
    return (grads.reshape(section_inputs.shape), first[None, None], second[None, None])


def solution(mesh):
    placed = (
        P("pipe", None, None, "tensor"),
        P(None, None, "tensor"),
        P("pipe", None, "tensor", None, None),
        P("pipe", None, "tensor", None, None),
        P("pipe", None),
        P("pipe", None, None),
    )
    return jax.shard_map(
        on_device,
        mesh=mesh,
        in_specs=placed,
        out_specs=(
            P("pipe", None, None, "tensor"),
            P("pipe", None, "tensor", None, None),
            P("pipe", None, "tensor", None, None),
        ),
        check_vma=False,
    )
```

```python
import jax
import jax.numpy as jnp
from jax import lax
from jax.experimental import pallas as pl
from jax.experimental.pallas import tpu as pltpu
from jax.sharding import PartitionSpec as P

gelu_scale = 0.7978845608028654
gelu_cubic = 0.044715
bf16 = jnp.bfloat16
f32 = jnp.float32
i32 = jnp.int32
sds = jax.ShapeDtypeStruct

NN = ((1,), (0,))
NT = ((1,), (1,))
LANES = 128
IDS = 64


def dot(left, right, dims):
    return lax.dot_general(left, right, (dims, ((), ())), preferred_element_type=f32)


def whole(space=pltpu.VMEM):
    return pl.BlockSpec(memory_space=space)


def gelu_pair(v):
    u = jnp.tanh(gelu_scale * (v + gelu_cubic * v * v * v))
    value = 0.5 * v * (1.0 + u)
    slope = 0.5 * (1.0 + u) + 0.5 * v * (1.0 - u * u) * gelu_scale * (1.0 + 3.0 * gelu_cubic * v * v)
    return value, slope


def prep_kernel(group_ref, drop_ref, perm_ref, w1_ref, w2_ref, packed_ref, w1d_ref, w2d_ref, pick1_ref, pick2_ref):
    groups, feats = perm_ref.shape
    blocks, size, _ = w1_ref.shape
    per_peer = feats // groups
    half = per_peer // 2
    own_group = group_ref[0]
    keep = drop_ref[0].astype(f32)
    base = own_group * feats
    rows = lax.broadcasted_iota(i32, (feats, feats), 0)
    cols = lax.broadcasted_iota(i32, (feats, feats), 1)
    before = jnp.where(rows < cols, 1.0, 0.0).astype(bf16)
    perm = perm_ref[...]
    mine = (perm >= base) & (perm < base + feats)
    rank = dot(jnp.where(mine, 1.0, 0.0).astype(bf16), before, NN)
    rank = jnp.where(mine, rank, -1.0).astype(i32)
    local = (perm - base).astype(f32)
    counter = lax.broadcasted_iota(i32, (half, feats), 0)
    lane = lax.broadcasted_iota(i32, (half, feats), 1)
    parts = []
    for part in range(2):
        for peer in range(groups):
            hit = counter + part * half == rank[peer : peer + 1, :]
            source = jnp.sum(jnp.where(hit, local[peer : peer + 1, :], 0.0), axis=1, keepdims=True)
            parts.append(jnp.where(lane == source.astype(i32), 1.0, 0.0))
    leave = jnp.concatenate(parts, axis=0).astype(bf16)
    own = perm_ref[pl.ds(own_group, 1), :]
    start = lax.broadcasted_iota(i32, (groups, feats), 0)
    from_group = (own >= start * feats) & (own < start * feats + feats)
    marks = jnp.where(from_group, 1.0, 0.0)
    place = dot(marks.astype(bf16), before, NN)
    place = place + jnp.where(place >= half, groups * half - half, 0.0) + start.astype(f32) * half
    slot = jnp.sum(marks * place, axis=0, keepdims=True).astype(i32)
    arrive = jnp.where(rows == slot, 1.0, 0.0)
    pick1_ref[...] = leave
    pick2_ref[...] = jnp.transpose(arrive).astype(bf16)
    arrive = arrive.astype(bf16)
    part1 = jnp.zeros((feats, size), f32)
    part2 = jnp.zeros((feats, size), f32)
    for block in range(blocks):
        span = slice(block * size, (block + 1) * size)
        one = dot(leave[:, span], w1_ref[block], NT)
        two = keep * dot(arrive[:, span], w2_ref[block], NN)
        w1d_ref[:, span] = one.astype(bf16)
        w2d_ref[:, span] = two.astype(bf16)
        part1 += one
        part2 += two
    packed_ref[0:feats, :] = part1.astype(bf16)
    packed_ref[feats : 2 * feats, :] = part2.astype(bf16)
    line = lax.broadcasted_iota(i32, (8, feats), 0)
    owner = (lax.broadcasted_iota(i32, (8, feats), 1) // size).astype(f32)
    ids = dot(jnp.where(line == 0, owner, 0.0).astype(bf16), leave, NT)
    ids += dot(jnp.where(line == 1, owner, 0.0).astype(bf16), arrive, NT)
    pieces = [ids[:, b * LANES : (b + 1) * LANES] for b in range(feats // LANES)]
    pieces.append(jnp.zeros((IDS - 8 * len(pieces), LANES), f32))
    packed_ref[2 * feats :, :] = jnp.concatenate(pieces, axis=0).astype(bf16)


def to_payload(values, ref):
    groups, _, parts, half, tokens = ref.shape
    for part in range(parts):
        span = values[part * groups * half : (part + 1) * groups * half]
        ref[:, 0, part] = span.reshape(groups, half, tokens).astype(bf16)


def from_payload(ref):
    groups, _, parts, half, tokens = ref.shape
    return jnp.concatenate(
        [ref[:, 0, part].astype(f32).reshape(groups * half, tokens) for part in range(parts)], axis=0
    )


def forward_kernel(x_ref, w1d_ref, hidden_ref, slope_ref):
    value, slope = gelu_pair(dot(w1d_ref[...], x_ref[0], NT))
    to_payload(value, hidden_ref)
    slope_ref[0] = slope


def settle_kernel(z_ref, x_ref, pick2_ref, z_out, x_out):
    z_out[0] = dot(pick2_ref[...], from_payload(z_ref).astype(bf16), NN).astype(bf16)
    x_out[0] = jnp.transpose(x_ref[0].astype(f32)).astype(bf16)


def expand_kernel(step_ref, first_ref, second_ref, x_ref, w1_ref, w2_ref, slope_ref):
    del step_ref
    feats = x_ref.shape[2]
    blocks = feats // LANES

    def owners(ref):
        ids = ref[0, 2 * feats :, :].astype(f32)
        return jnp.transpose(jnp.concatenate([ids[8 * b : 8 * b + 8] for b in range(blocks)], axis=1))

    one = first_ref[0, 0:feats, :].astype(f32)
    two = second_ref[0, feats : 2 * feats, :].astype(f32)
    own1 = owners(first_ref)[:, 0:1]
    own2 = owners(second_ref)[:, 1:2]
    for b in range(blocks):
        span = slice(b * LANES, (b + 1) * LANES)
        w1_ref[:, span] = jnp.where(own1 == b, one, 0.0).astype(bf16)
        w2_ref[:, span] = jnp.where(own2 == b, two, 0.0).astype(bf16)
    v = dot(x_ref[0], w1_ref[...], NT)
    _, slope = gelu_pair(jnp.concatenate([v[:, : feats // 2], v[:, feats // 2 :]], axis=0))
    slope_ref[...] = slope


def mix(g, w2_ref, mixed_ref):
    feats = g.shape[1]
    s = dot(g, w2_ref[...], NT)
    s = jnp.concatenate([s[:, : feats // 2], s[:, feats // 2 :]], axis=0)
    mixed_ref[...] = jnp.transpose(s).reshape(mixed_ref.shape).astype(bf16)


def start_kernel(g_ref, packed_ref, stored_ref, mixed_ref, w2_ref):
    feats = g_ref.shape[1]
    blocks = feats // LANES
    ids = packed_ref[0, 2 * feats :, :].astype(f32)
    own = jnp.transpose(jnp.concatenate([ids[8 * b : 8 * b + 8] for b in range(blocks)], axis=1))[:, 1:2]
    two = packed_ref[0, feats : 2 * feats, :].astype(f32)
    for b in range(blocks):
        w2_ref[:, b * LANES : (b + 1) * LANES] = jnp.where(own == b, two, 0.0).astype(bf16)
    g = g_ref[...]
    stored_ref[0] = g
    mix(g, w2_ref, mixed_ref)


def relay_kernel(step_ref, returned_ref, g_in_ref, slope_ref, w1_ref, w2_ref, old_ref, stored_ref, g_ref, mixed_ref):
    del step_ref, old_ref
    groups, half, lanes = returned_ref.shape
    tokens = lanes // 2
    dh = returned_ref[...].astype(f32).reshape(groups * half, lanes)
    da = (jnp.transpose(dh) * slope_ref[...]).astype(bf16)
    g = g_in_ref[...].astype(f32)
    g = g + (dot(da[:tokens], w1_ref[: groups * half], NN) + dot(da[tokens:], w1_ref[groups * half :], NN))
    g = g.astype(bf16)
    stored_ref[0] = g
    g_ref[...] = g
    mix(g, w2_ref, mixed_ref)


def owner_send_kernel(g_ref, w2d_ref, mixed_ref):
    to_payload(dot(w2d_ref[...], g_ref[0], NT), mixed_ref)


def owner_kernel(drop_ref, returned_ref, slope_ref, pick1_ref, w1_ref, x_ref, z_ref, g_ref, grads_ref, first_ref, second_ref):
    blocks, size, _ = first_ref.shape
    keep = drop_ref[0].astype(f32)
    da = jnp.transpose(from_payload(returned_ref) * slope_ref[0]).astype(bf16)
    da = dot(da, pick1_ref[...], NN).astype(bf16)

    @pl.when(pl.program_id(0) == 0)
    def _():
        first_ref[...] = jnp.zeros_like(first_ref)
        second_ref[...] = jnp.zeros_like(second_ref)

    for block in range(blocks):
        span = slice(block * size, (block + 1) * size)
        g = g_ref[0, :, span]
        grads_ref[0, :, span] = (g.astype(f32) + dot(da[:, span], w1_ref[block], NT)).astype(bf16)
        first_ref[block] += dot(x_ref[0, span, :], da[:, span], NN)
        second_ref[block] += keep * dot(z_ref[0, span, :], g, NN)


def on_device(section_inputs, out_grad, w_first, w_second, drop_flags, perm):
    sections = lax.axis_size("pipe")
    row = lax.axis_index("pipe").astype(i32)
    groups = lax.axis_size("tensor")
    group = lax.axis_index("tensor").astype(i32)
    x = section_inputs[0]
    micros, tokens, feats = x.shape
    share = micros * tokens // sections
    blocks, size = w_first.shape[2], w_first.shape[3]
    half = feats // groups // 2
    drop = drop_flags.reshape(1)
    params = pltpu.CompilerParams(vmem_limit_bytes=60 * 1024 * 1024)
    square = sds((feats, feats), bf16)

    xs = lax.all_to_all(x.reshape(sections, share, feats), "pipe", 0, 0, tiled=True)

    packed, w1d, w2d, pick1, pick2 = pl.pallas_call(
        prep_kernel,
        in_specs=[whole(pltpu.SMEM), whole(pltpu.SMEM), whole(), whole(), whole()],
        out_specs=[whole()] * 5,
        out_shape=[sds((2 * feats + IDS, LANES), bf16)] + [square] * 4,
        compiler_params=params,
        name="prep",
    )(group.reshape(1), drop, perm.reshape(groups, feats), w_first[0, 0], w_second[0, 0])
    packed = lax.all_gather(packed, "pipe")

    payload = sds((groups, micros, 2, half, tokens), bf16)
    payload_spec = pl.BlockSpec((groups, 1, 2, half, tokens), lambda m: (0, m, 0, 0, 0))
    token_spec = pl.BlockSpec((1, tokens, feats), lambda m: (m, 0, 0))
    feature_spec = pl.BlockSpec((1, feats, tokens), lambda m: (m, 0, 0))
    square_spec = pl.BlockSpec((feats, feats), lambda m: (0, 0))
    weight_spec = pl.BlockSpec((blocks, size, size), lambda m: (0, 0, 0))

    hidden, slope = pl.pallas_call(
        forward_kernel,
        grid=(micros,),
        in_specs=[token_spec, square_spec],
        out_specs=[payload_spec, feature_spec],
        out_shape=[payload, sds((micros, feats, tokens), f32)],
        compiler_params=params,
        name="forward",
    )(x, w1d)
    hidden, xs = lax.optimization_barrier((hidden, xs))
    z = lax.all_to_all(hidden, "tensor", 0, 0, tiled=True)

    mixed_shape = sds((groups, half, 2 * share), bf16)
    value_shape = sds((share, feats), bf16)
    stored_shape = sds((sections, share, feats), bf16)
    pack_rows = 2 * feats + IDS
    own_grad = lax.dynamic_index_in_dim(out_grad.reshape(sections, share, feats), row, 0, keepdims=False)
    own_grad, z = lax.optimization_barrier((own_grad, z))
    g = own_grad
    stored, mixed = pl.pallas_call(
        start_kernel,
        grid=(1,),
        in_specs=[
            pl.BlockSpec((share, feats), lambda i: (0, 0)),
            pl.BlockSpec((1, pack_rows, LANES), lambda i: (sections - 1, 0, 0)),
        ],
        out_specs=[
            pl.BlockSpec((1, share, feats), lambda i: (sections - 1, 0, 0)),
            pl.BlockSpec((groups, half, 2 * share), lambda i: (0, 0, 0)),
        ],
        out_shape=[stored_shape, mixed_shape],
        scratch_shapes=[pltpu.VMEM((feats, feats), bf16)],
        compiler_params=params,
        name="start",
    )(g, packed)

    expand = pl.pallas_call(
        expand_kernel,
        grid_spec=pltpu.PrefetchScalarGridSpec(
            num_scalar_prefetch=1,
            grid=(1,),
            in_specs=[
                pl.BlockSpec((1, pack_rows, LANES), lambda i, s: (s[0], 0, 0)),
                pl.BlockSpec((1, pack_rows, LANES), lambda i, s: (s[0] - 1, 0, 0)),
                pl.BlockSpec((1, share, feats), lambda i, s: (s[0], 0, 0)),
            ],
            out_specs=[
                pl.BlockSpec((feats, feats), lambda i, s: (0, 0)),
                pl.BlockSpec((feats, feats), lambda i, s: (0, 0)),
                pl.BlockSpec((2 * share, feats // 2), lambda i, s: (0, 0)),
            ],
        ),
        out_shape=[square, square, sds((2 * share, feats // 2), f32)],
        compiler_params=params,
        name="expand",
    )
    relay = pl.pallas_call(
        relay_kernel,
        grid_spec=pltpu.PrefetchScalarGridSpec(
            num_scalar_prefetch=1,
            grid=(1,),
            in_specs=[whole()] * 5 + [whole(pl.ANY)],
            out_specs=[
                pl.BlockSpec((1, share, feats), lambda i, s: (s[0] - 1, 0, 0)),
                whole(),
                whole(),
            ],
        ),
        out_shape=[stored_shape, value_shape, mixed_shape],
        input_output_aliases={6: 0},
        compiler_params=params,
        name="relay",
    )

    def advance(k, carry):
        g, mixed, stored = carry
        at = jnp.full((1,), sections - 1 - k, i32)
        returned = lax.all_to_all(mixed, "tensor", 0, 0, tiled=True)
        w1, w2, scale = expand(at, packed, packed, xs)
        stored, g, mixed = relay(at, returned, g, scale, w1, w2, stored)
        return (g, mixed, stored)

    _, _, stored = lax.fori_loop(0, sections - 1, advance, (g, mixed, stored))
    stored, z = lax.optimization_barrier((stored, z))
    cotangent = lax.all_to_all(stored, "pipe", 0, 0, tiled=True)
    cotangent = cotangent.reshape(micros, tokens, feats)
    z, x_turned = pl.pallas_call(
        settle_kernel,
        grid=(micros,),
        in_specs=[payload_spec, token_spec, square_spec],
        out_specs=[feature_spec, feature_spec],
        out_shape=[sds((micros, feats, tokens), bf16)] * 2,
        compiler_params=params,
        name="settle",
    )(z, x, pick2)

    mixed = pl.pallas_call(
        owner_send_kernel,
        grid=(micros,),
        in_specs=[token_spec, square_spec],
        out_specs=payload_spec,
        out_shape=payload,
        compiler_params=params,
        name="owner_send",
    )(cotangent, w2d)
    returned = lax.all_to_all(mixed, "tensor", 0, 0, tiled=True)
    grads, first, second = pl.pallas_call(
        owner_kernel,
        grid=(micros,),
        in_specs=[
            whole(pltpu.SMEM),
            payload_spec,
            feature_spec,
            square_spec,
            weight_spec,
            feature_spec,
            feature_spec,
            token_spec,
        ],
        out_specs=[token_spec, weight_spec, weight_spec],
        out_shape=[sds(x.shape, bf16), sds((blocks, size, size), f32), sds((blocks, size, size), f32)],
        compiler_params=params,
        name="owner",
    )(drop, returned, slope, pick1, w_first[0, 0], x_turned, z, cotangent)
    return (grads[None], first[None, None], second[None, None])


def solution(mesh):
    placed = (
        P("pipe", None, None, "tensor"),
        P(None, None, "tensor"),
        P("pipe", None, "tensor", None, None),
        P("pipe", None, "tensor", None, None),
        P("pipe", None),
        P("pipe", None, None),
    )
    return jax.shard_map(
        on_device,
        mesh=mesh,
        in_specs=placed,
        out_specs=(
            P("pipe", None, None, "tensor"),
            P("pipe", None, "tensor", None, None),
            P("pipe", None, "tensor", None, None),
        ),
        check_vma=False,
    )
```

```python
import jax
import jax.numpy as jnp
from jax import lax
from jax.experimental import pallas as pl
from jax.experimental.pallas import tpu as pltpu
from jax.sharding import PartitionSpec as P

gelu_scale = 0.7978845608028654
gelu_cubic = 0.044715
bf16 = jnp.bfloat16
f32 = jnp.float32
i32 = jnp.int32
sds = jax.ShapeDtypeStruct

NN = ((1,), (0,))
NT = ((1,), (1,))
LANES = 128
IDS = 64


def dot(left, right, dims):
    return lax.dot_general(left, right, (dims, ((), ())), preferred_element_type=f32)


def whole(space=pltpu.VMEM):
    return pl.BlockSpec(memory_space=space)


def gelu_pair(v):
    u = jnp.tanh(gelu_scale * (v + gelu_cubic * v * v * v))
    value = 0.5 * v * (1.0 + u)
    slope = 0.5 * (1.0 + u) + 0.5 * v * (1.0 - u * u) * gelu_scale * (1.0 + 3.0 * gelu_cubic * v * v)
    return value, slope


def prep_kernel(group_ref, drop_ref, perm_ref, w1_ref, w2_ref, packed1_ref, packed2_ref, w1d_ref, w2d_ref, pick1_ref, pick2_ref):
    feats = pick1_ref.shape[0]
    groups = perm_ref.shape[1] // feats
    blocks, size, _ = w1_ref.shape
    per_peer = feats // groups
    half = per_peer // 2
    own_group = group_ref[0]
    keep = drop_ref[0].astype(f32)
    base = own_group * feats
    rows = lax.broadcasted_iota(i32, (feats, feats), 0)
    cols = lax.broadcasted_iota(i32, (feats, feats), 1)
    before = jnp.where(rows < cols, 1.0, 0.0).astype(bf16)
    perm = jnp.concatenate([perm_ref[:, g * feats : (g + 1) * feats] for g in range(groups)], axis=0)
    mine = (perm >= base) & (perm < base + feats)
    rank = dot(jnp.where(mine, 1.0, 0.0).astype(bf16), before, NN)
    rank = jnp.where(mine, rank, -1.0).astype(i32)
    local = (perm - base).astype(f32)
    counter = lax.broadcasted_iota(i32, (half, feats), 0)
    lane = lax.broadcasted_iota(i32, (half, feats), 1)
    parts = []
    for part in range(2):
        for peer in range(groups):
            hit = counter + part * half == rank[peer : peer + 1, :]
            source = jnp.sum(jnp.where(hit, local[peer : peer + 1, :], 0.0), axis=1, keepdims=True)
            parts.append(jnp.where(lane == source.astype(i32), 1.0, 0.0))
    leave = jnp.concatenate(parts, axis=0).astype(bf16)
    start = lax.broadcasted_iota(i32, (groups, feats), 0)
    own = jnp.sum(jnp.where(start == own_group, perm, 0), axis=0, keepdims=True)
    from_group = (own >= start * feats) & (own < start * feats + feats)
    marks = jnp.where(from_group, 1.0, 0.0)
    place = dot(marks.astype(bf16), before, NN)
    place = place + jnp.where(place >= half, groups * half - half, 0.0) + start.astype(f32) * half
    slot = jnp.sum(marks * place, axis=0, keepdims=True).astype(i32)
    arrive = jnp.where(rows == slot, 1.0, 0.0)
    pick1_ref[...] = leave
    pick2_ref[...] = jnp.transpose(arrive).astype(bf16)
    arrive = arrive.astype(bf16)
    part1 = jnp.zeros((feats, size), f32)
    part2 = jnp.zeros((feats, size), f32)
    for block in range(blocks):
        span = slice(block * size, (block + 1) * size)
        one = dot(leave[:, span], w1_ref[block], NT)
        two = keep * dot(arrive[:, span], w2_ref[block], NN)
        w1d_ref[:, span] = one.astype(bf16)
        w2d_ref[:, span] = two.astype(bf16)
        part1 += one
        part2 += two
    packed1_ref[0:feats, :] = part1.astype(bf16)
    packed2_ref[0:feats, :] = part2.astype(bf16)
    line = lax.broadcasted_iota(i32, (8, feats), 0)
    owner = (lax.broadcasted_iota(i32, (8, feats), 1) // size).astype(f32)
    owner = jnp.where(line == 0, owner, 0.0).astype(bf16)
    for ref, chosen in ((packed1_ref, leave), (packed2_ref, arrive)):
        ids = dot(owner, chosen, NT)
        pieces = [ids[:, b * LANES : (b + 1) * LANES] for b in range(feats // LANES)]
        pieces.append(jnp.zeros((IDS - 8 * len(pieces), LANES), f32))
        ref[feats:, :] = jnp.concatenate(pieces, axis=0).astype(bf16)


def to_payload(values, ref):
    groups, _, parts, half, tokens = ref.shape
    for part in range(parts):
        span = values[part * groups * half : (part + 1) * groups * half]
        ref[:, 0, part] = span.reshape(groups, half, tokens).astype(bf16)


def from_payload(ref):
    groups, _, parts, half, tokens = ref.shape
    return jnp.concatenate(
        [ref[:, 0, part].astype(f32).reshape(groups * half, tokens) for part in range(parts)], axis=0
    )


def forward_kernel(x_ref, w1d_ref, hidden_ref, slope_ref):
    value, slope = gelu_pair(dot(w1d_ref[...], x_ref[0], NT))
    to_payload(value, hidden_ref)
    slope_ref[0] = slope


def settle_kernel(z_ref, x_ref, pick2_ref, z_out, x_out):
    z_out[0] = dot(pick2_ref[...], from_payload(z_ref).astype(bf16), NN).astype(bf16)
    x_out[0] = jnp.transpose(x_ref[0].astype(f32)).astype(bf16)


def spread(packed_ref, dense_ref):
    feats = dense_ref.shape[0]
    blocks = feats // LANES
    ids = packed_ref[0, feats:, :].astype(f32)
    own = jnp.transpose(jnp.concatenate([ids[8 * b : 8 * b + 8] for b in range(blocks)], axis=1))[:, 0:1]
    values = packed_ref[0, 0:feats, :].astype(f32)
    for b in range(blocks):
        dense_ref[:, b * LANES : (b + 1) * LANES] = jnp.where(own == b, values, 0.0).astype(bf16)


def expand_kernel(step_ref, first_ref, second_ref, x_ref, w1_ref, w2_ref, slope_ref):
    del step_ref
    feats = x_ref.shape[2]
    spread(first_ref, w1_ref)
    spread(second_ref, w2_ref)
    v = dot(x_ref[0], w1_ref[...], NT)
    _, slope = gelu_pair(jnp.concatenate([v[:, : feats // 2], v[:, feats // 2 :]], axis=0))
    slope_ref[...] = slope


def mix(g, w2_ref, mixed_ref, ready=(None, None)):
    feats = g.shape[1]
    pieces = []
    for part, wait in enumerate(ready):
        if wait is not None:
            wait.wait()
        pieces.append(dot(g, w2_ref[part * (feats // 2) : (part + 1) * (feats // 2), :], NT))
    s = jnp.concatenate(pieces, axis=0)
    mixed_ref[...] = jnp.transpose(s).reshape(mixed_ref.shape).astype(bf16)


def start_kernel(g_ref, packed_ref, mixed_ref, w2_ref):
    spread(packed_ref, w2_ref)
    mix(g_ref[...], w2_ref, mixed_ref)


def relay_kernel(returned_ref, g_in_ref, slope_hbm, w1_hbm, w2_hbm, g_ref, mixed_ref, slope_ref, w1_ref, w2_ref, sems):
    groups, half, lanes = returned_ref.shape
    tokens = lanes // 2
    split = groups * half
    upper, lower = pl.ds(0, split), pl.ds(split, split)
    slope_copy = pltpu.make_async_copy(slope_hbm, slope_ref, sems.at[0])
    copies = [
        pltpu.make_async_copy(source.at[span], target.at[span], sems.at[1 + index])
        for index, (source, target, span) in enumerate(
            [(w1_hbm, w1_ref, upper), (w1_hbm, w1_ref, lower), (w2_hbm, w2_ref, upper), (w2_hbm, w2_ref, lower)]
        )
    ]
    slope_copy.start()
    for copy in copies:
        copy.start()
    dh = jnp.transpose(returned_ref[...].astype(f32).reshape(split, lanes))
    slope_copy.wait()
    da = (dh * slope_ref[...]).astype(bf16)
    copies[0].wait()
    term = dot(da[:tokens], w1_ref[:split], NN)
    copies[1].wait()
    term = term + dot(da[tokens:], w1_ref[split:], NN)
    g = (g_in_ref[...].astype(f32) + term).astype(bf16)
    g_ref[...] = g
    mix(g, w2_ref, mixed_ref, copies[2:])


def owner_send_kernel(g_ref, w2d_ref, mixed_ref):
    to_payload(dot(w2d_ref[...], g_ref[0], NT), mixed_ref)


def owner_kernel(drop_ref, returned_ref, slope_ref, pick1_ref, w1_ref, x_ref, z_ref, g_ref, grads_ref, first_ref, second_ref):
    blocks, size, _ = first_ref.shape
    keep = drop_ref[0].astype(f32)
    da = jnp.transpose(from_payload(returned_ref) * slope_ref[0]).astype(bf16)
    da = dot(da, pick1_ref[...], NN).astype(bf16)

    @pl.when(pl.program_id(0) == 0)
    def _():
        first_ref[...] = jnp.zeros_like(first_ref)
        second_ref[...] = jnp.zeros_like(second_ref)

    for block in range(blocks):
        span = slice(block * size, (block + 1) * size)
        g = g_ref[0, :, span]
        grads_ref[0, :, span] = (g.astype(f32) + dot(da[:, span], w1_ref[block], NT)).astype(bf16)
        first_ref[block] += dot(x_ref[0, span, :], da[:, span], NN)
        second_ref[block] += keep * dot(z_ref[0, span, :], g, NN)


def on_device(section_inputs, out_grad, w_first, w_second, drop_flags, perm):
    sections = lax.axis_size("pipe")
    row = lax.axis_index("pipe").astype(i32)
    groups = lax.axis_size("tensor")
    group = lax.axis_index("tensor").astype(i32)
    feats = section_inputs.shape[3]
    tokens = 2 * section_inputs.shape[2]
    micros = section_inputs.shape[1] // 2
    x = section_inputs.reshape(micros, tokens, feats)
    share = micros * tokens // sections
    blocks, size = w_first.shape[2], w_first.shape[3]
    half = feats // groups // 2
    drop = drop_flags.reshape(1)
    params = pltpu.CompilerParams(vmem_limit_bytes=60 * 1024 * 1024)
    square = sds((feats, feats), bf16)
    pack_rows = feats + IDS

    xs = lax.all_to_all(x.reshape(sections, share, feats), "pipe", 0, 0, tiled=True)

    packed1, packed2, w1d, w2d, pick1, pick2 = pl.pallas_call(
        prep_kernel,
        in_specs=[whole(pltpu.SMEM), whole(pltpu.SMEM), whole(), whole(), whole()],
        out_specs=[whole()] * 6,
        out_shape=[sds((pack_rows, LANES), bf16)] * 2 + [square] * 4,
        compiler_params=params,
        name="prep",
    )(group.reshape(1), drop, perm[0], w_first[0, 0], w_second[0, 0])
    packed2 = lax.all_gather(packed2, "pipe")
    packed1 = lax.all_gather(packed1, "pipe")

    payload = sds((groups, micros, 2, half, tokens), bf16)
    payload_spec = pl.BlockSpec((groups, 1, 2, half, tokens), lambda m: (0, m, 0, 0, 0))
    token_spec = pl.BlockSpec((1, tokens, feats), lambda m: (m, 0, 0))
    feature_spec = pl.BlockSpec((1, feats, tokens), lambda m: (m, 0, 0))
    square_spec = pl.BlockSpec((feats, feats), lambda m: (0, 0))
    weight_spec = pl.BlockSpec((blocks, size, size), lambda m: (0, 0, 0))

    hidden, slope = pl.pallas_call(
        forward_kernel,
        grid=(micros,),
        in_specs=[token_spec, square_spec],
        out_specs=[payload_spec, feature_spec],
        out_shape=[payload, sds((micros, feats, tokens), f32)],
        compiler_params=params,
        name="forward",
    )(x, w1d)
    mixed_shape = sds((groups, half, 2 * share), bf16)
    value_shape = sds((share, feats), bf16)
    g = lax.dynamic_index_in_dim(out_grad.reshape(sections, share, feats), row, 0, keepdims=False)
    mixed = pl.pallas_call(
        start_kernel,
        grid=(1,),
        in_specs=[
            pl.BlockSpec((share, feats), lambda i: (0, 0)),
            pl.BlockSpec((1, pack_rows, LANES), lambda i: (sections - 1, 0, 0)),
        ],
        out_specs=pl.BlockSpec((groups, half, 2 * share), lambda i: (0, 0, 0)),
        out_shape=mixed_shape,
        scratch_shapes=[pltpu.VMEM((feats, feats), bf16)],
        compiler_params=params,
        name="start",
    )(g, packed2)
    mixed, xs = lax.optimization_barrier((mixed, xs))
    returned = lax.all_to_all(mixed, "tensor", 0, 0, tiled=True)
    returned, hidden = lax.optimization_barrier((returned, hidden))
    z = lax.all_to_all(hidden, "tensor", 0, 0, tiled=True)
    returned, z = lax.optimization_barrier((returned, z))

    expand = pl.pallas_call(
        expand_kernel,
        grid_spec=pltpu.PrefetchScalarGridSpec(
            num_scalar_prefetch=1,
            grid=(1,),
            in_specs=[
                pl.BlockSpec((1, pack_rows, LANES), lambda i, s: (s[0], 0, 0)),
                pl.BlockSpec((1, pack_rows, LANES), lambda i, s: (s[0] - 1, 0, 0)),
                pl.BlockSpec((1, share, feats), lambda i, s: (s[0], 0, 0)),
            ],
            out_specs=[
                pl.BlockSpec((feats, feats), lambda i, s: (0, 0)),
                pl.BlockSpec((feats, feats), lambda i, s: (0, 0)),
                pl.BlockSpec((2 * share, feats // 2), lambda i, s: (0, 0)),
            ],
        ),
        out_shape=[square, square, sds((2 * share, feats // 2), f32)],
        compiler_params=params,
        name="expand",
    )
    relay = pl.pallas_call(
        relay_kernel,
        in_specs=[whole()] * 2 + [whole(pltpu.HBM)] * 3,
        out_specs=[whole()] * 2,
        out_shape=[value_shape, mixed_shape],
        scratch_shapes=[
            pltpu.VMEM((2 * share, feats // 2), f32),
            pltpu.VMEM((feats, feats), bf16),
            pltpu.VMEM((feats, feats), bf16),
            pltpu.SemaphoreType.DMA((5,)),
        ],
        compiler_params=pltpu.CompilerParams(vmem_limit_bytes=60 * 1024 * 1024),
        name="relay",
    )

    def prepare(s):
        return expand(jnp.full((1,), s, i32), packed1, packed2, xs)

    w1, w2, scale = prepare(sections - 1)
    stored = jnp.zeros((sections, share, feats), bf16)
    stored = lax.dynamic_update_index_in_dim(stored, g, sections - 1, 0)
    g, mixed = relay(returned, g, scale, w1, w2)

    def advance(k, carry):
        g, mixed, stored = carry
        s = sections - 2 - k
        returned = lax.all_to_all(mixed, "tensor", 0, 0, tiled=True)
        stored = lax.dynamic_update_index_in_dim(stored, g, s, 0)
        w1, w2, scale = prepare(s)
        g, mixed = relay(returned, g, scale, w1, w2)
        return (g, mixed, stored)

    g, _, stored = lax.fori_loop(0, sections - 2, advance, (g, mixed, stored))
    stored = lax.dynamic_update_index_in_dim(stored, g, 0, 0)
    stored, z = lax.optimization_barrier((stored, z))
    cotangent = lax.all_to_all(stored, "pipe", 0, 0, tiled=True)
    cotangent = cotangent.reshape(micros, tokens, feats)
    z, x_turned = pl.pallas_call(
        settle_kernel,
        grid=(micros,),
        in_specs=[payload_spec, token_spec, square_spec],
        out_specs=[feature_spec, feature_spec],
        out_shape=[sds((micros, feats, tokens), bf16)] * 2,
        compiler_params=params,
        name="settle",
    )(z, x, pick2)

    mixed = pl.pallas_call(
        owner_send_kernel,
        grid=(micros,),
        in_specs=[token_spec, square_spec],
        out_specs=payload_spec,
        out_shape=payload,
        compiler_params=params,
        name="owner_send",
    )(cotangent, w2d)
    returned = lax.all_to_all(mixed, "tensor", 0, 0, tiled=True)
    grads, first, second = pl.pallas_call(
        owner_kernel,
        grid=(micros,),
        in_specs=[
            whole(pltpu.SMEM),
            payload_spec,
            feature_spec,
            square_spec,
            weight_spec,
            feature_spec,
            feature_spec,
            token_spec,
        ],
        out_specs=[token_spec, weight_spec, weight_spec],
        out_shape=[sds(x.shape, bf16), sds((blocks, size, size), f32), sds((blocks, size, size), f32)],
        compiler_params=params,
        name="owner",
    )(drop, returned, slope, pick1, w_first[0, 0], x_turned, z, cotangent)
    return (grads.reshape(section_inputs.shape), first[None, None], second[None, None])


def solution(mesh):
    placed = (
        P("pipe", None, None, "tensor"),
        P(None, None, "tensor"),
        P("pipe", None, "tensor", None, None),
        P("pipe", None, "tensor", None, None),
        P("pipe", None),
        P("pipe", None, None),
    )
    return jax.shard_map(
        on_device,
        mesh=mesh,
        in_specs=placed,
        out_specs=(
            P("pipe", None, None, "tensor"),
            P("pipe", None, "tensor", None, None),
            P("pipe", None, "tensor", None, None),
        ),
        check_vma=False,
    )
```

```python
import jax
import jax.numpy as jnp
from jax import lax
from jax.experimental import pallas as pl
from jax.experimental.pallas import tpu as pltpu
from jax.sharding import PartitionSpec as P

gelu_scale = 0.7978845608028654
gelu_cubic = 0.044715
bf16 = jnp.bfloat16
f32 = jnp.float32
i32 = jnp.int32
sds = jax.ShapeDtypeStruct

NN = ((1,), (0,))
NT = ((1,), (1,))
LANES = 128
IDS = 16
RELAY_MIB = 16
EXPAND_MIB = 16


def dot(left, right, dims):
    return lax.dot_general(left, right, (dims, ((), ())), preferred_element_type=f32)


def whole(space=pltpu.VMEM):
    return pl.BlockSpec(memory_space=space)


def gelu_pair(v):
    u = jnp.tanh(gelu_scale * (v + gelu_cubic * v * v * v))
    value = 0.5 * v * (1.0 + u)
    slope = 0.5 * (1.0 + u) + 0.5 * v * (1.0 - u * u) * gelu_scale * (1.0 + 3.0 * gelu_cubic * v * v)
    return value, slope


def prep_kernel(group_ref, drop_ref, perm_ref, w1_ref, w2_ref, packed_ref, w1d_ref, w2d_ref, pick1_ref, pick2_ref):
    feats = pick1_ref.shape[0]
    groups = perm_ref.shape[1] // feats
    blocks, size, _ = w1_ref.shape
    per_peer = feats // groups
    half = per_peer // 2
    own_group = group_ref[0]
    keep = drop_ref[0].astype(f32)
    base = own_group * feats
    rows = lax.broadcasted_iota(i32, (feats, feats), 0)
    cols = lax.broadcasted_iota(i32, (feats, feats), 1)
    before = jnp.where(rows < cols, 1.0, 0.0).astype(bf16)
    perm = jnp.concatenate([perm_ref[:, g * feats : (g + 1) * feats] for g in range(groups)], axis=0)
    mine = (perm >= base) & (perm < base + feats)
    rank = dot(jnp.where(mine, 1.0, 0.0).astype(bf16), before, NN)
    rank = jnp.where(mine, rank, -1.0).astype(i32)
    local = (perm - base).astype(f32)
    counter = lax.broadcasted_iota(i32, (half, feats), 0)
    lane = lax.broadcasted_iota(i32, (half, feats), 1)
    parts = []
    for part in range(2):
        for peer in range(groups):
            hit = counter + part * half == rank[peer : peer + 1, :]
            source = jnp.sum(jnp.where(hit, local[peer : peer + 1, :], 0.0), axis=1, keepdims=True)
            parts.append(jnp.where(lane == source.astype(i32), 1.0, 0.0))
    leave = jnp.concatenate(parts, axis=0).astype(bf16)
    start = lax.broadcasted_iota(i32, (groups, feats), 0)
    own = jnp.sum(jnp.where(start == own_group, perm, 0), axis=0, keepdims=True)
    from_group = (own >= start * feats) & (own < start * feats + feats)
    marks = jnp.where(from_group, 1.0, 0.0)
    place = dot(marks.astype(bf16), before, NN)
    place = place + jnp.where(place >= half, groups * half - half, 0.0) + start.astype(f32) * half
    slot = jnp.sum(marks * place, axis=0, keepdims=True).astype(i32)
    arrive = jnp.where(rows == slot, 1.0, 0.0)
    pick1_ref[...] = leave
    arrive_t = jnp.transpose(arrive).astype(bf16)
    pick2_ref[...] = arrive_t
    arrive = arrive.astype(bf16)
    part1 = jnp.zeros((size, feats), f32)
    part2 = jnp.zeros((size, feats), f32)
    for block in range(blocks):
        span = slice(block * size, (block + 1) * size)
        w1d_ref[:, span] = dot(leave[:, span], w1_ref[block], NT).astype(bf16)
        w2d_ref[:, span] = (keep * dot(arrive[:, span], w2_ref[block], NN)).astype(bf16)
        part1 += dot(w1_ref[block], leave[:, span], NT)
        part2 += keep * dot(jnp.transpose(w2_ref[block].astype(f32)).astype(bf16), arrive_t[span, :], NN)
    packed_ref[0:size, :] = part1.astype(bf16)
    packed_ref[size : 2 * size, :] = part2.astype(bf16)
    line = lax.broadcasted_iota(i32, (IDS, feats), 0)
    owner = (lax.broadcasted_iota(i32, (IDS, feats), 1) // size).astype(f32)
    ids = dot(jnp.where(line == 0, owner, 0.0).astype(bf16), leave, NT)
    ids += dot(jnp.where(line == 1, owner, 0.0).astype(bf16), arrive, NT)
    packed_ref[2 * size :, :] = ids.astype(bf16)


def to_payload(values, ref):
    groups, _, parts, half, tokens = ref.shape
    for part in range(parts):
        span = values[part * groups * half : (part + 1) * groups * half]
        ref[:, 0, part] = span.reshape(groups, half, tokens).astype(bf16)


def from_payload(ref):
    groups, _, parts, half, tokens = ref.shape
    return jnp.concatenate(
        [ref[:, 0, part].astype(f32).reshape(groups * half, tokens) for part in range(parts)], axis=0
    )


def forward_kernel(x_ref, w1d_ref, hidden_ref, slope_ref):
    value, slope = gelu_pair(dot(w1d_ref[...], x_ref[0], NT))
    to_payload(value, hidden_ref)
    slope_ref[0] = slope


def settle_kernel(z_ref, x_ref, pick2_ref, z_out, x_out):
    z_out[0] = dot(pick2_ref[...], from_payload(z_ref).astype(bf16), NN).astype(bf16)
    x_out[0] = jnp.transpose(x_ref[0].astype(f32)).astype(bf16)


def spread(values, ids, dense_ref):
    size = values.shape[0]
    for b in range(dense_ref.shape[0] // size):
        dense_ref[b * size : (b + 1) * size, :] = jnp.where(ids == b, values, 0.0).astype(bf16)


def expand_kernel(step_ref, first_ref, second_ref, x_ref, w1_ref, w2_ref, slope_ref):
    del step_ref
    feats = x_ref.shape[2]
    first = first_ref[0].astype(f32)
    spread(first[:LANES], first[2 * LANES : 2 * LANES + 1], w1_ref)
    w2_ref[...] = second_ref[0, LANES:, :]
    v = dot(x_ref[0], w1_ref[...], NN)
    _, slope = gelu_pair(jnp.concatenate([v[:, : feats // 2], v[:, feats // 2 :]], axis=0))
    slope_ref[...] = slope


def mix(g, w2_ref, mixed_ref):
    feats = g.shape[1]
    s = dot(g, w2_ref[...], NN)
    s = jnp.concatenate([s[:, : feats // 2], s[:, feats // 2 :]], axis=0)
    mixed_ref[...] = jnp.transpose(s).reshape(mixed_ref.shape).astype(bf16)


def start_kernel(g_ref, packed_ref, mixed_ref, w2_ref):
    packed = packed_ref[0].astype(f32)
    spread(packed[LANES : 2 * LANES], packed[2 * LANES + 1 : 2 * LANES + 2], w2_ref)
    mix(g_ref[...], w2_ref, mixed_ref)


def relay_kernel(returned_ref, g_in_ref, slope_ref, w1_ref, packed_ref, g_ref, mixed_ref, w2_ref):
    packed = packed_ref[...].astype(f32)
    spread(packed[:LANES], packed[LANES + 1 : LANES + 2], w2_ref)
    groups, half, lanes = returned_ref.shape
    tokens = lanes // 2
    dh = returned_ref[...].astype(f32).reshape(groups * half, lanes)
    da = (jnp.transpose(dh) * slope_ref[...]).astype(bf16)
    da = jnp.concatenate([da[:tokens], da[tokens:]], axis=1)
    g = (g_in_ref[...].astype(f32) + dot(da, w1_ref[...], NT)).astype(bf16)
    g_ref[...] = g
    mix(g, w2_ref, mixed_ref)


def owner_send_kernel(g_ref, w2d_ref, mixed_ref):
    to_payload(dot(w2d_ref[...], g_ref[0], NT), mixed_ref)


def owner_kernel(drop_ref, returned_ref, slope_ref, pick1_ref, w1_ref, x_ref, z_ref, g_ref, grads_ref, first_ref, second_ref):
    blocks, size, _ = first_ref.shape
    keep = drop_ref[0].astype(f32)
    da = jnp.transpose(from_payload(returned_ref) * slope_ref[0]).astype(bf16)
    da = dot(da, pick1_ref[...], NN).astype(bf16)

    @pl.when(pl.program_id(0) == 0)
    def _():
        first_ref[...] = jnp.zeros_like(first_ref)
        second_ref[...] = jnp.zeros_like(second_ref)

    for block in range(blocks):
        span = slice(block * size, (block + 1) * size)
        g = g_ref[0, :, span]
        grads_ref[0, :, span] = (g.astype(f32) + dot(da[:, span], w1_ref[block], NT)).astype(bf16)
        first_ref[block] += dot(x_ref[0, span, :], da[:, span], NN)
        second_ref[block] += keep * dot(z_ref[0, span, :], g, NN)


def on_device(section_inputs, out_grad, w_first, w_second, drop_flags, perm):
    sections = lax.axis_size("pipe")
    row = lax.axis_index("pipe").astype(i32)
    groups = lax.axis_size("tensor")
    group = lax.axis_index("tensor").astype(i32)
    feats = section_inputs.shape[3]
    tokens = 2 * section_inputs.shape[2]
    micros = section_inputs.shape[1] // 2
    x = section_inputs.reshape(micros, tokens, feats)
    share = micros * tokens // sections
    blocks, size = w_first.shape[2], w_first.shape[3]
    half = feats // groups // 2
    drop = drop_flags.reshape(1)
    params = pltpu.CompilerParams(vmem_limit_bytes=60 * 1024 * 1024)
    square = sds((feats, feats), bf16)
    pack_rows = 2 * LANES + IDS

    xs = lax.all_to_all(x.reshape(sections, share, feats), "pipe", 0, 0, tiled=True)

    packed, w1d, w2d, pick1, pick2 = pl.pallas_call(
        prep_kernel,
        in_specs=[whole(pltpu.SMEM), whole(pltpu.SMEM), whole(), whole(), whole()],
        out_specs=[whole()] * 5,
        out_shape=[sds((pack_rows, feats), bf16)] + [square] * 4,
        compiler_params=params,
        name="prep",
    )(group.reshape(1), drop, perm[0], w_first[0, 0], w_second[0, 0])
    packed, xs = lax.optimization_barrier((packed, xs))
    packed = lax.all_gather(packed, "pipe")

    payload = sds((groups, micros, 2, half, tokens), bf16)
    payload_spec = pl.BlockSpec((groups, 1, 2, half, tokens), lambda m: (0, m, 0, 0, 0))
    token_spec = pl.BlockSpec((1, tokens, feats), lambda m: (m, 0, 0))
    feature_spec = pl.BlockSpec((1, feats, tokens), lambda m: (m, 0, 0))
    square_spec = pl.BlockSpec((feats, feats), lambda m: (0, 0))
    weight_spec = pl.BlockSpec((blocks, size, size), lambda m: (0, 0, 0))

    hidden, slope = pl.pallas_call(
        forward_kernel,
        grid=(micros,),
        in_specs=[token_spec, square_spec],
        out_specs=[payload_spec, feature_spec],
        out_shape=[payload, sds((micros, feats, tokens), f32)],
        compiler_params=params,
        name="forward",
    )(x, w1d)
    mixed_shape = sds((groups, half, 2 * share), bf16)
    value_shape = sds((share, feats), bf16)
    g = lax.dynamic_index_in_dim(out_grad.reshape(sections, share, feats), row, 0, keepdims=False)
    mixed = pl.pallas_call(
        start_kernel,
        grid=(1,),
        in_specs=[
            pl.BlockSpec((share, feats), lambda i: (0, 0)),
            pl.BlockSpec((1, pack_rows, feats), lambda i: (sections - 1, 0, 0)),
        ],
        out_specs=pl.BlockSpec((groups, half, 2 * share), lambda i: (0, 0, 0)),
        out_shape=mixed_shape,
        scratch_shapes=[pltpu.VMEM((feats, feats), bf16)],
        compiler_params=params,
        name="start",
    )(g, packed)
    hidden, xs = lax.optimization_barrier((hidden, xs))
    z = lax.all_to_all(hidden, "tensor", 0, 0, tiled=True)
    mixed, z = lax.optimization_barrier((mixed, z))
    returned = lax.all_to_all(mixed, "tensor", 0, 0, tiled=True)

    expand = pl.pallas_call(
        expand_kernel,
        grid_spec=pltpu.PrefetchScalarGridSpec(
            num_scalar_prefetch=1,
            grid=(1,),
            in_specs=[
                pl.BlockSpec((1, pack_rows, feats), lambda i, s: (s[0], 0, 0)),
                pl.BlockSpec((1, pack_rows, feats), lambda i, s: (s[0] - 1, 0, 0)),
                pl.BlockSpec((1, share, feats), lambda i, s: (s[0], 0, 0)),
            ],
            out_specs=[whole()] * 3,
        ),
        out_shape=[square, sds((pack_rows - LANES, feats), bf16), sds((2 * share, feats // 2), f32)],
        compiler_params=pltpu.CompilerParams(vmem_limit_bytes=EXPAND_MIB * 1024 * 1024),
        name="expand",
    )
    relay = pl.pallas_call(
        relay_kernel,
        in_specs=[whole()] * 5,
        out_specs=[whole()] * 2,
        out_shape=[value_shape, mixed_shape],
        scratch_shapes=[pltpu.VMEM((feats, feats), bf16)],
        compiler_params=pltpu.CompilerParams(vmem_limit_bytes=RELAY_MIB * 1024 * 1024),
        name="relay",
    )

    def prepare(s):
        return expand(jnp.full((1,), s, i32), packed, packed, xs)

    w1, w2, scale = prepare(sections - 1)
    stored = jnp.zeros((sections, share, feats), bf16)
    stored = lax.dynamic_update_index_in_dim(stored, g, sections - 1, 0)
    g, mixed = relay(returned, g, scale, w1, w2)

    def advance(k, carry):
        g, mixed, stored = carry
        s = sections - 2 - k
        returned = lax.all_to_all(mixed, "tensor", 0, 0, tiled=True)
        stored = lax.dynamic_update_index_in_dim(stored, g, s, 0)
        w1, w2, scale = prepare(s)
        g, mixed = relay(returned, g, scale, w1, w2)
        return (g, mixed, stored)

    g, _, stored = lax.fori_loop(0, sections - 2, advance, (g, mixed, stored))
    stored = lax.dynamic_update_index_in_dim(stored, g, 0, 0)
    stored, z = lax.optimization_barrier((stored, z))
    cotangent = lax.all_to_all(stored, "pipe", 0, 0, tiled=True)
    cotangent = cotangent.reshape(micros, tokens, feats)
    z, x_turned = pl.pallas_call(
        settle_kernel,
        grid=(micros,),
        in_specs=[payload_spec, token_spec, square_spec],
        out_specs=[feature_spec, feature_spec],
        out_shape=[sds((micros, feats, tokens), bf16)] * 2,
        compiler_params=params,
        name="settle",
    )(z, x, pick2)

    mixed = pl.pallas_call(
        owner_send_kernel,
        grid=(micros,),
        in_specs=[token_spec, square_spec],
        out_specs=payload_spec,
        out_shape=payload,
        compiler_params=params,
        name="owner_send",
    )(cotangent, w2d)
    returned = lax.all_to_all(mixed, "tensor", 0, 0, tiled=True)
    grads, first, second = pl.pallas_call(
        owner_kernel,
        grid=(micros,),
        in_specs=[
            whole(pltpu.SMEM),
            payload_spec,
            feature_spec,
            square_spec,
            weight_spec,
            feature_spec,
            feature_spec,
            token_spec,
        ],
        out_specs=[token_spec, weight_spec, weight_spec],
        out_shape=[sds(x.shape, bf16), sds((blocks, size, size), f32), sds((blocks, size, size), f32)],
        compiler_params=params,
        name="owner",
    )(drop, returned, slope, pick1, w_first[0, 0], x_turned, z, cotangent)
    return (grads.reshape(section_inputs.shape), first[None, None], second[None, None])


def solution(mesh):
    placed = (
        P("pipe", None, None, "tensor"),
        P(None, None, "tensor"),
        P("pipe", None, "tensor", None, None),
        P("pipe", None, "tensor", None, None),
        P("pipe", None),
        P("pipe", None, None),
    )
    return jax.shard_map(
        on_device,
        mesh=mesh,
        in_specs=placed,
        out_specs=(
            P("pipe", None, None, "tensor"),
            P("pipe", None, "tensor", None, None),
            P("pipe", None, "tensor", None, None),
        ),
        check_vma=False,
    )
```

```python
import jax
import jax.numpy as jnp
from jax import lax
from jax.experimental import pallas as pl
from jax.experimental.pallas import tpu as pltpu
from jax.sharding import PartitionSpec as P

gelu_scale = 0.7978845608028654
gelu_cubic = 0.044715
bf16 = jnp.bfloat16
f32 = jnp.float32
i32 = jnp.int32
sds = jax.ShapeDtypeStruct

NN = ((1,), (0,))
NT = ((1,), (1,))
LANES = 128
IDS = 16
OWNER_MIB = 52
RELAY_MIB = 16
EXPAND_MIB = 16


def dot(left, right, dims):
    return lax.dot_general(left, right, (dims, ((), ())), preferred_element_type=f32)


def whole(space=pltpu.VMEM):
    return pl.BlockSpec(memory_space=space)


def gelu_pair(v):
    u = jnp.tanh(gelu_scale * (v + gelu_cubic * v * v * v))
    value = 0.5 * v * (1.0 + u)
    slope = 0.5 * (1.0 + u) + 0.5 * v * (1.0 - u * u) * gelu_scale * (1.0 + 3.0 * gelu_cubic * v * v)
    return value, slope


def prep_kernel(group_ref, drop_ref, perm_ref, w1_ref, w2_ref, packed_ref, w1d_ref, w2d_ref, pick1_ref, pick2_ref):
    feats = pick1_ref.shape[0]
    groups = perm_ref.shape[1] // feats
    blocks, size, _ = w1_ref.shape
    per_peer = feats // groups
    half = per_peer // 2
    own_group = group_ref[0]
    keep = drop_ref[0].astype(f32)
    base = own_group * feats
    rows = lax.broadcasted_iota(i32, (feats, feats), 0)
    cols = lax.broadcasted_iota(i32, (feats, feats), 1)
    before = jnp.where(rows < cols, 1.0, 0.0).astype(bf16)
    perm = jnp.concatenate([perm_ref[:, g * feats : (g + 1) * feats] for g in range(groups)], axis=0)
    mine = (perm >= base) & (perm < base + feats)
    rank = dot(jnp.where(mine, 1.0, 0.0).astype(bf16), before, NN)
    rank = jnp.where(mine, rank, -1.0).astype(i32)
    local = (perm - base).astype(f32)
    counter = lax.broadcasted_iota(i32, (half, feats), 0)
    lane = lax.broadcasted_iota(i32, (half, feats), 1)
    parts = []
    for part in range(2):
        for peer in range(groups):
            hit = counter + part * half == rank[peer : peer + 1, :]
            source = jnp.sum(jnp.where(hit, local[peer : peer + 1, :], 0.0), axis=1, keepdims=True)
            parts.append(jnp.where(lane == source.astype(i32), 1.0, 0.0))
    leave = jnp.concatenate(parts, axis=0).astype(bf16)
    start = lax.broadcasted_iota(i32, (groups, feats), 0)
    own = jnp.sum(jnp.where(start == own_group, perm, 0), axis=0, keepdims=True)
    from_group = (own >= start * feats) & (own < start * feats + feats)
    marks = jnp.where(from_group, 1.0, 0.0)
    place = dot(marks.astype(bf16), before, NN)
    place = place + jnp.where(place >= half, groups * half - half, 0.0) + start.astype(f32) * half
    slot = jnp.sum(marks * place, axis=0, keepdims=True).astype(i32)
    arrive = jnp.where(rows == slot, 1.0, 0.0)
    pick1_ref[...] = leave
    arrive_t = jnp.transpose(arrive).astype(bf16)
    pick2_ref[...] = arrive_t
    arrive = arrive.astype(bf16)
    part1 = jnp.zeros((size, feats), f32)
    part2 = jnp.zeros((size, feats), f32)
    for block in range(blocks):
        span = slice(block * size, (block + 1) * size)
        w1d_ref[:, span] = dot(leave[:, span], w1_ref[block], NT).astype(bf16)
        w2d_ref[:, span] = (keep * dot(arrive[:, span], w2_ref[block], NN)).astype(bf16)
        part1 += dot(w1_ref[block], leave[:, span], NT)
        part2 += keep * dot(jnp.transpose(w2_ref[block].astype(f32)).astype(bf16), arrive_t[span, :], NN)
    packed_ref[0:size, :] = part1.astype(bf16)
    packed_ref[size : 2 * size, :] = part2.astype(bf16)
    line = lax.broadcasted_iota(i32, (IDS, feats), 0)
    owner = (lax.broadcasted_iota(i32, (IDS, feats), 1) // size).astype(f32)
    ids = dot(jnp.where(line == 0, owner, 0.0).astype(bf16), leave, NT)
    ids += dot(jnp.where(line == 1, owner, 0.0).astype(bf16), arrive, NT)
    packed_ref[2 * size :, :] = ids.astype(bf16)


def to_payload(values, ref):
    groups, _, parts, half, tokens = ref.shape
    for part in range(parts):
        span = values[part * groups * half : (part + 1) * groups * half]
        ref[:, 0, part] = span.reshape(groups, half, tokens).astype(bf16)


def from_payload(ref):
    groups, _, parts, half, tokens = ref.shape
    return jnp.concatenate(
        [ref[:, 0, part].astype(f32).reshape(groups * half, tokens) for part in range(parts)], axis=0
    )


def forward_kernel(x_ref, w1d_ref, hidden_ref, slope_ref):
    value, slope = gelu_pair(dot(w1d_ref[...], x_ref[0], NT))
    to_payload(value, hidden_ref)
    slope_ref[0] = slope


def settle_kernel(z_ref, x_ref, pick2_ref, z_out, x_out):
    z_out[0] = dot(pick2_ref[...], from_payload(z_ref).astype(bf16), NN).astype(bf16)
    x_out[0] = jnp.transpose(x_ref[0].astype(f32)).astype(bf16)


def spread(values, ids, dense_ref):
    size = values.shape[0]
    for b in range(dense_ref.shape[0] // size):
        dense_ref[b * size : (b + 1) * size, :] = jnp.where(ids == b, values, 0.0).astype(bf16)


def expand_kernel(step_ref, first_ref, second_ref, x_ref, w1_ref, w2_ref, slope_ref):
    del step_ref
    feats = x_ref.shape[2]
    first = first_ref[0].astype(f32)
    spread(first[:LANES], first[2 * LANES : 2 * LANES + 1], w1_ref)
    w2_ref[...] = second_ref[0, LANES:, :]
    v = dot(x_ref[0], w1_ref[...], NN)
    _, slope = gelu_pair(jnp.concatenate([v[:, : feats // 2], v[:, feats // 2 :]], axis=0))
    slope_ref[...] = slope


def mix(g, w2_ref, mixed_ref):
    feats = g.shape[1]
    s = dot(g, w2_ref[...], NN)
    s = jnp.concatenate([s[:, : feats // 2], s[:, feats // 2 :]], axis=0)
    mixed_ref[...] = jnp.transpose(s).reshape(mixed_ref.shape).astype(bf16)


def start_kernel(g_ref, packed_ref, mixed_ref, w2_ref):
    packed = packed_ref[0].astype(f32)
    spread(packed[LANES : 2 * LANES], packed[2 * LANES + 1 : 2 * LANES + 2], w2_ref)
    mix(g_ref[...], w2_ref, mixed_ref)


def relay_kernel(returned_ref, g_in_ref, slope_ref, w1_ref, packed_ref, g_ref, mixed_ref, w2_ref):
    packed = packed_ref[...].astype(f32)
    spread(packed[:LANES], packed[LANES + 1 : LANES + 2], w2_ref)
    groups, half, lanes = returned_ref.shape
    tokens = lanes // 2
    dh = returned_ref[...].astype(f32).reshape(groups * half, lanes)
    da = (jnp.transpose(dh) * slope_ref[...]).astype(bf16)
    da = jnp.concatenate([da[:tokens], da[tokens:]], axis=1)
    g = (g_in_ref[...].astype(f32) + dot(da, w1_ref[...], NT)).astype(bf16)
    g_ref[...] = g
    mix(g, w2_ref, mixed_ref)


def owner_send_kernel(g_ref, w2d_ref, mixed_ref):
    to_payload(dot(w2d_ref[...], g_ref[0], NT), mixed_ref)


def owner_kernel(drop_ref, returned_ref, slope_ref, pick1_ref, w1_ref, x_ref, z_ref, g_ref, grads_ref, first_ref, second_ref):
    blocks, size, _ = first_ref.shape
    keep = drop_ref[0].astype(f32)
    da = jnp.transpose(from_payload(returned_ref) * slope_ref[0]).astype(bf16)
    da = dot(da, pick1_ref[...], NN).astype(bf16)

    @pl.when(pl.program_id(0) == 0)
    def _():
        first_ref[...] = jnp.zeros_like(first_ref)
        second_ref[...] = jnp.zeros_like(second_ref)

    for block in range(blocks):
        span = slice(block * size, (block + 1) * size)
        g = g_ref[0, :, span]
        grads_ref[0, :, span] = (g.astype(f32) + dot(da[:, span], w1_ref[block], NT)).astype(bf16)
        first_ref[block] += dot(x_ref[0, span, :], da[:, span], NN)
        second_ref[block] += keep * dot(z_ref[0, span, :], g, NN)


def on_device(section_inputs, out_grad, w_first, w_second, drop_flags, perm):
    sections = lax.axis_size("pipe")
    row = lax.axis_index("pipe").astype(i32)
    groups = lax.axis_size("tensor")
    group = lax.axis_index("tensor").astype(i32)
    feats = section_inputs.shape[3]
    tokens = 2 * section_inputs.shape[2]
    micros = section_inputs.shape[1] // 2
    x = section_inputs.reshape(micros, tokens, feats)
    share = micros * tokens // sections
    blocks, size = w_first.shape[2], w_first.shape[3]
    half = feats // groups // 2
    drop = drop_flags.reshape(1)
    params = pltpu.CompilerParams(vmem_limit_bytes=60 * 1024 * 1024)
    square = sds((feats, feats), bf16)
    pack_rows = 2 * LANES + IDS

    packed, w1d, w2d, pick1, pick2 = pl.pallas_call(
        prep_kernel,
        in_specs=[whole(pltpu.SMEM), whole(pltpu.SMEM), whole(), whole(), whole()],
        out_specs=[whole()] * 5,
        out_shape=[sds((pack_rows, feats), bf16)] + [square] * 4,
        compiler_params=params,
        name="prep",
    )(group.reshape(1), drop, perm[0], w_first[0, 0], w_second[0, 0])
    packed = lax.all_gather(packed, "pipe")

    payload = sds((groups, micros, 2, half, tokens), bf16)
    payload_spec = pl.BlockSpec((groups, 1, 2, half, tokens), lambda m: (0, m, 0, 0, 0))
    token_spec = pl.BlockSpec((1, tokens, feats), lambda m: (m, 0, 0))
    feature_spec = pl.BlockSpec((1, feats, tokens), lambda m: (m, 0, 0))
    square_spec = pl.BlockSpec((feats, feats), lambda m: (0, 0))
    weight_spec = pl.BlockSpec((blocks, size, size), lambda m: (0, 0, 0))

    hidden, slope = pl.pallas_call(
        forward_kernel,
        grid=(micros,),
        in_specs=[token_spec, square_spec],
        out_specs=[payload_spec, feature_spec],
        out_shape=[payload, sds((micros, feats, tokens), f32)],
        compiler_params=params,
        name="forward",
    )(x, w1d)
    mixed_shape = sds((groups, half, 2 * share), bf16)
    value_shape = sds((share, feats), bf16)
    g = lax.dynamic_index_in_dim(out_grad.reshape(sections, share, feats), row, 0, keepdims=False)
    mixed = pl.pallas_call(
        start_kernel,
        grid=(1,),
        in_specs=[
            pl.BlockSpec((share, feats), lambda i: (0, 0)),
            pl.BlockSpec((1, pack_rows, feats), lambda i: (sections - 1, 0, 0)),
        ],
        out_specs=pl.BlockSpec((groups, half, 2 * share), lambda i: (0, 0, 0)),
        out_shape=mixed_shape,
        scratch_shapes=[pltpu.VMEM((feats, feats), bf16)],
        compiler_params=params,
        name="start",
    )(g, packed)
    z = lax.all_to_all(hidden, "tensor", 0, 0, tiled=True)
    to_share, z = lax.optimization_barrier((x, z))
    xs = lax.all_to_all(to_share.reshape(sections, share, feats), "pipe", 0, 0, tiled=True)
    mixed, xs = lax.optimization_barrier((mixed, xs))
    returned = lax.all_to_all(mixed, "tensor", 0, 0, tiled=True)

    expand = pl.pallas_call(
        expand_kernel,
        grid_spec=pltpu.PrefetchScalarGridSpec(
            num_scalar_prefetch=1,
            grid=(1,),
            in_specs=[
                pl.BlockSpec((1, pack_rows, feats), lambda i, s: (s[0], 0, 0)),
                pl.BlockSpec((1, pack_rows, feats), lambda i, s: (s[0] - 1, 0, 0)),
                pl.BlockSpec((1, share, feats), lambda i, s: (s[0], 0, 0)),
            ],
            out_specs=[whole()] * 3,
        ),
        out_shape=[square, sds((pack_rows - LANES, feats), bf16), sds((2 * share, feats // 2), f32)],
        compiler_params=pltpu.CompilerParams(vmem_limit_bytes=EXPAND_MIB * 1024 * 1024),
        name="expand",
    )
    relay = pl.pallas_call(
        relay_kernel,
        in_specs=[whole()] * 5,
        out_specs=[whole()] * 2,
        out_shape=[value_shape, mixed_shape],
        scratch_shapes=[pltpu.VMEM((feats, feats), bf16)],
        compiler_params=pltpu.CompilerParams(vmem_limit_bytes=RELAY_MIB * 1024 * 1024),
        name="relay",
    )

    def prepare(s):
        return expand(jnp.full((1,), s, i32), packed, packed, xs)

    w1, w2, scale = prepare(sections - 1)
    stored = jnp.zeros((sections, share, feats), bf16)
    stored = lax.dynamic_update_index_in_dim(stored, g, sections - 1, 0)
    g, mixed = relay(returned, g, scale, w1, w2)

    def advance(k, carry):
        g, mixed, stored = carry
        s = sections - 2 - k
        returned = lax.all_to_all(mixed, "tensor", 0, 0, tiled=True)
        stored = lax.dynamic_update_index_in_dim(stored, g, s, 0)
        w1, w2, scale = prepare(s)
        g, mixed = relay(returned, g, scale, w1, w2)
        return (g, mixed, stored)

    g, _, stored = lax.fori_loop(0, sections - 2, advance, (g, mixed, stored))
    stored = lax.dynamic_update_index_in_dim(stored, g, 0, 0)
    stored, z = lax.optimization_barrier((stored, z))
    cotangent = lax.all_to_all(stored, "pipe", 0, 0, tiled=True)
    cotangent = cotangent.reshape(micros, tokens, feats)
    z, x_turned = pl.pallas_call(
        settle_kernel,
        grid=(micros,),
        in_specs=[payload_spec, token_spec, square_spec],
        out_specs=[feature_spec, feature_spec],
        out_shape=[sds((micros, feats, tokens), bf16)] * 2,
        compiler_params=params,
        name="settle",
    )(z, x, pick2)

    mixed = pl.pallas_call(
        owner_send_kernel,
        grid=(micros,),
        in_specs=[token_spec, square_spec],
        out_specs=payload_spec,
        out_shape=payload,
        compiler_params=params,
        name="owner_send",
    )(cotangent, w2d)
    returned = lax.all_to_all(mixed, "tensor", 0, 0, tiled=True)
    grads, first, second = pl.pallas_call(
        owner_kernel,
        grid=(micros,),
        in_specs=[
            whole(pltpu.SMEM),
            payload_spec,
            feature_spec,
            square_spec,
            weight_spec,
            feature_spec,
            feature_spec,
            token_spec,
        ],
        out_specs=[token_spec, weight_spec, weight_spec],
        out_shape=[sds(x.shape, bf16), sds((blocks, size, size), f32), sds((blocks, size, size), f32)],
        compiler_params=pltpu.CompilerParams(vmem_limit_bytes=OWNER_MIB * 1024 * 1024),
        name="owner",
    )(drop, returned, slope, pick1, w_first[0, 0], x_turned, z, cotangent)
    return (grads.reshape(section_inputs.shape), first[None, None], second[None, None])


def solution(mesh):
    placed = (
        P("pipe", None, None, "tensor"),
        P(None, None, "tensor"),
        P("pipe", None, "tensor", None, None),
        P("pipe", None, "tensor", None, None),
        P("pipe", None),
        P("pipe", None, None),
    )
    return jax.shard_map(
        on_device,
        mesh=mesh,
        in_specs=placed,
        out_specs=(
            P("pipe", None, None, "tensor"),
            P("pipe", None, "tensor", None, None),
            P("pipe", None, "tensor", None, None),
        ),
        check_vma=False,
    )
```

```python
import jax
import jax.numpy as jnp
from jax import lax
from jax.experimental import pallas as pl
from jax.experimental.pallas import tpu as pltpu
from jax.sharding import PartitionSpec as P

gelu_scale = 0.7978845608028654
gelu_cubic = 0.044715
bf16 = jnp.bfloat16
f32 = jnp.float32
i32 = jnp.int32
sds = jax.ShapeDtypeStruct

NN = ((1,), (0,))
NT = ((1,), (1,))
LANES = 128
IDS = 16
OWNER_MIB = 52
RELAY_MIB = 16
EXPAND_MIB = 16


def dot(left, right, dims):
    return lax.dot_general(left, right, (dims, ((), ())), preferred_element_type=f32)


def whole(space=pltpu.VMEM):
    return pl.BlockSpec(memory_space=space)


def gelu_pair(v):
    u = jnp.tanh(gelu_scale * (v + gelu_cubic * v * v * v))
    value = 0.5 * v * (1.0 + u)
    slope = 0.5 * (1.0 + u) + 0.5 * v * (1.0 - u * u) * gelu_scale * (1.0 + 3.0 * gelu_cubic * v * v)
    return value, slope


def prep_kernel(group_ref, drop_ref, perm_ref, w1_ref, w2_ref, packed_ref, w1d_ref, w2d_ref, pick1_ref, pick2_ref):
    feats = pick1_ref.shape[0]
    groups = perm_ref.shape[1] // feats
    blocks, size, _ = w1_ref.shape
    per_peer = feats // groups
    half = per_peer // 2
    own_group = group_ref[0]
    keep = drop_ref[0].astype(f32)
    base = own_group * feats
    rows = lax.broadcasted_iota(i32, (feats, feats), 0)
    cols = lax.broadcasted_iota(i32, (feats, feats), 1)
    before = jnp.where(rows < cols, 1.0, 0.0).astype(bf16)
    perm = jnp.concatenate([perm_ref[:, g * feats : (g + 1) * feats] for g in range(groups)], axis=0)
    mine = (perm >= base) & (perm < base + feats)
    rank = dot(jnp.where(mine, 1.0, 0.0).astype(bf16), before, NN)
    rank = jnp.where(mine, rank, -1.0).astype(i32)
    local = (perm - base).astype(f32)
    counter = lax.broadcasted_iota(i32, (half, feats), 0)
    lane = lax.broadcasted_iota(i32, (half, feats), 1)
    parts = []
    for part in range(2):
        for peer in range(groups):
            hit = counter + part * half == rank[peer : peer + 1, :]
            source = jnp.sum(jnp.where(hit, local[peer : peer + 1, :], 0.0), axis=1, keepdims=True)
            parts.append(jnp.where(lane == source.astype(i32), 1.0, 0.0))
    leave = jnp.concatenate(parts, axis=0).astype(bf16)
    start = lax.broadcasted_iota(i32, (groups, feats), 0)
    own = jnp.sum(jnp.where(start == own_group, perm, 0), axis=0, keepdims=True)
    from_group = (own >= start * feats) & (own < start * feats + feats)
    marks = jnp.where(from_group, 1.0, 0.0)
    place = dot(marks.astype(bf16), before, NN)
    place = place + jnp.where(place >= half, groups * half - half, 0.0) + start.astype(f32) * half
    slot = jnp.sum(marks * place, axis=0, keepdims=True).astype(i32)
    arrive = jnp.where(rows == slot, 1.0, 0.0)
    pick1_ref[...] = leave
    arrive_t = jnp.transpose(arrive).astype(bf16)
    pick2_ref[...] = arrive_t
    arrive = arrive.astype(bf16)
    part1 = jnp.zeros((size, feats), f32)
    part2 = jnp.zeros((size, feats), f32)
    for block in range(blocks):
        span = slice(block * size, (block + 1) * size)
        w1d_ref[:, span] = dot(leave[:, span], w1_ref[block], NT).astype(bf16)
        w2d_ref[:, span] = (keep * dot(arrive[:, span], w2_ref[block], NN)).astype(bf16)
        part1 += dot(w1_ref[block], leave[:, span], NT)
        part2 += keep * dot(jnp.transpose(w2_ref[block].astype(f32)).astype(bf16), arrive_t[span, :], NN)
    packed_ref[0:size, :] = part1.astype(bf16)
    packed_ref[size : 2 * size, :] = part2.astype(bf16)
    line = lax.broadcasted_iota(i32, (IDS, feats), 0)
    owner = (lax.broadcasted_iota(i32, (IDS, feats), 1) // size).astype(f32)
    ids = dot(jnp.where(line == 0, owner, 0.0).astype(bf16), leave, NT)
    ids += dot(jnp.where(line == 1, owner, 0.0).astype(bf16), arrive, NT)
    packed_ref[2 * size :, :] = ids.astype(bf16)


def to_payload(values, ref):
    groups, _, parts, half, tokens = ref.shape
    for part in range(parts):
        span = values[part * groups * half : (part + 1) * groups * half]
        ref[:, 0, part] = span.reshape(groups, half, tokens).astype(bf16)


def from_payload(ref):
    groups, _, parts, half, tokens = ref.shape
    return jnp.concatenate(
        [ref[:, 0, part].astype(f32).reshape(groups * half, tokens) for part in range(parts)], axis=0
    )


def forward_kernel(x_ref, w1d_ref, hidden_ref, slope_ref):
    value, slope = gelu_pair(dot(w1d_ref[...], x_ref[0], NT))
    to_payload(value, hidden_ref)
    slope_ref[0] = slope


def settle_kernel(z_ref, x_ref, pick2_ref, z_out, x_out):
    z_out[0] = dot(pick2_ref[...], from_payload(z_ref).astype(bf16), NN).astype(bf16)
    x_out[0] = jnp.transpose(x_ref[0].astype(f32)).astype(bf16)


def spread(values, ids, dense_ref):
    size = values.shape[0]
    for b in range(dense_ref.shape[0] // size):
        dense_ref[b * size : (b + 1) * size, :] = jnp.where(ids == b, values, 0.0).astype(bf16)


def expand_kernel(step_ref, table_ref, first_ref, second_ref, x_ref, w1_ref, w2_ref, slope_ref):
    del step_ref
    feats = x_ref.shape[2]
    first = first_ref[0].astype(f32)
    spread(first[:LANES], first[2 * LANES : 2 * LANES + 1], w1_ref)
    w2_ref[...] = second_ref[0, LANES:, :]
    v = dot(x_ref[0], w1_ref[...], NN)
    _, slope = gelu_pair(jnp.concatenate([v[:, : feats // 2], v[:, feats // 2 :]], axis=0))
    slope_ref[...] = slope


def mix(g, w2_ref, mixed_ref):
    feats = g.shape[1]
    s = dot(g, w2_ref[...], NN)
    s = jnp.concatenate([s[:, : feats // 2], s[:, feats // 2 :]], axis=0)
    mixed_ref[...] = jnp.transpose(s).reshape(mixed_ref.shape).astype(bf16)


def start_kernel(table_ref, g_ref, packed_ref, mixed_ref, w2_ref):
    packed = packed_ref[0].astype(f32)
    spread(packed[LANES : 2 * LANES], packed[2 * LANES + 1 : 2 * LANES + 2], w2_ref)
    mix(g_ref[...], w2_ref, mixed_ref)


def relay_kernel(returned_ref, g_in_ref, slope_ref, w1_ref, packed_ref, g_ref, mixed_ref, w2_ref):
    packed = packed_ref[...].astype(f32)
    spread(packed[:LANES], packed[LANES + 1 : LANES + 2], w2_ref)
    groups, half, lanes = returned_ref.shape
    tokens = lanes // 2
    dh = returned_ref[...].astype(f32).reshape(groups * half, lanes)
    da = (jnp.transpose(dh) * slope_ref[...]).astype(bf16)
    da = jnp.concatenate([da[:tokens], da[tokens:]], axis=1)
    g = (g_in_ref[...].astype(f32) + dot(da, w1_ref[...], NT)).astype(bf16)
    g_ref[...] = g
    mix(g, w2_ref, mixed_ref)


def owner_send_kernel(g_ref, w2d_ref, mixed_ref):
    to_payload(dot(w2d_ref[...], g_ref[0], NT), mixed_ref)


def owner_kernel(drop_ref, returned_ref, slope_ref, pick1_ref, w1_ref, x_ref, z_ref, g_ref, grads_ref, first_ref, second_ref):
    blocks, size, _ = first_ref.shape
    keep = drop_ref[0].astype(f32)
    da = jnp.transpose(from_payload(returned_ref) * slope_ref[0]).astype(bf16)
    da = dot(da, pick1_ref[...], NN).astype(bf16)

    @pl.when(pl.program_id(0) == 0)
    def _():
        first_ref[...] = jnp.zeros_like(first_ref)
        second_ref[...] = jnp.zeros_like(second_ref)

    for block in range(blocks):
        span = slice(block * size, (block + 1) * size)
        g = g_ref[0, :, span]
        grads_ref[0, :, span] = (g.astype(f32) + dot(da[:, span], w1_ref[block], NT)).astype(bf16)
        first_ref[block] += dot(x_ref[0, span, :], da[:, span], NN)
        second_ref[block] += keep * dot(z_ref[0, span, :], g, NN)


def on_device(section_inputs, out_grad, w_first, w_second, drop_flags, perm):
    sections = lax.axis_size("pipe")
    row = lax.axis_index("pipe").astype(i32)
    groups = lax.axis_size("tensor")
    group = lax.axis_index("tensor").astype(i32)
    feats = section_inputs.shape[3]
    tokens = 2 * section_inputs.shape[2]
    micros = section_inputs.shape[1] // 2
    x = section_inputs.reshape(micros, tokens, feats)
    share = micros * tokens // sections
    blocks, size = w_first.shape[2], w_first.shape[3]
    half = feats // groups // 2
    drop = drop_flags.reshape(1)
    params = pltpu.CompilerParams(vmem_limit_bytes=60 * 1024 * 1024)
    square = sds((feats, feats), bf16)
    pack_rows = 2 * LANES + IDS

    packed, w1d, w2d, pick1, pick2 = pl.pallas_call(
        prep_kernel,
        in_specs=[whole(pltpu.SMEM), whole(pltpu.SMEM), whole(), whole(), whole()],
        out_specs=[whole()] * 5,
        out_shape=[sds((pack_rows, feats), bf16)] + [square] * 4,
        compiler_params=params,
        name="prep",
    )(group.reshape(1), drop, perm[0], w_first[0, 0], w_second[0, 0])
    chips = sections // 2
    core, chip = row % 2, row // 2
    swap = [(i, i ^ 1) for i in range(sections)]
    onward = [(2 * z, 2 * ((z + 1) % chips)) for z in range(chips)]
    onward += [(2 * z + 1, 2 * ((z - 1) % chips) + 1) for z in range(chips)]
    other = lax.ppermute(packed, "pipe", swap)
    current = jnp.stack([jnp.where(core == 0, packed, other), jnp.where(core == 0, other, packed)])
    places = [current] + [None] * (chips - 1)
    for distance in range(1, chips // 2 + 1):
        current = lax.ppermute(current, "pipe", onward)
        places[chips - distance] = current
        if 2 * distance < chips:
            places[distance] = lax.ppermute(current, "pipe", swap)
    packed = jnp.stack(places).reshape(sections, pack_rows, feats)
    index = jnp.arange(sections, dtype=i32)
    table = ((1 - 2 * core) * (index // 2 - chip)) % chips * 2 + index % 2

    payload = sds((groups, micros, 2, half, tokens), bf16)
    payload_spec = pl.BlockSpec((groups, 1, 2, half, tokens), lambda m: (0, m, 0, 0, 0))
    token_spec = pl.BlockSpec((1, tokens, feats), lambda m: (m, 0, 0))
    feature_spec = pl.BlockSpec((1, feats, tokens), lambda m: (m, 0, 0))
    square_spec = pl.BlockSpec((feats, feats), lambda m: (0, 0))
    weight_spec = pl.BlockSpec((blocks, size, size), lambda m: (0, 0, 0))

    hidden, slope = pl.pallas_call(
        forward_kernel,
        grid=(micros,),
        in_specs=[token_spec, square_spec],
        out_specs=[payload_spec, feature_spec],
        out_shape=[payload, sds((micros, feats, tokens), f32)],
        compiler_params=params,
        name="forward",
    )(x, w1d)
    mixed_shape = sds((groups, half, 2 * share), bf16)
    value_shape = sds((share, feats), bf16)
    g = lax.dynamic_index_in_dim(out_grad.reshape(sections, share, feats), row, 0, keepdims=False)
    mixed = pl.pallas_call(
        start_kernel,
        grid_spec=pltpu.PrefetchScalarGridSpec(
            num_scalar_prefetch=1,
            grid=(1,),
            in_specs=[
                pl.BlockSpec((share, feats), lambda i, t: (0, 0)),
                pl.BlockSpec((1, pack_rows, feats), lambda i, t: (t[sections - 1], 0, 0)),
            ],
            out_specs=pl.BlockSpec((groups, half, 2 * share), lambda i, t: (0, 0, 0)),
            scratch_shapes=[pltpu.VMEM((feats, feats), bf16)],
        ),
        out_shape=mixed_shape,
        compiler_params=params,
        name="start",
    )(table, g, packed)
    z = lax.all_to_all(hidden, "tensor", 0, 0, tiled=True)
    to_share, z = lax.optimization_barrier((x, z))
    xs = lax.all_to_all(to_share.reshape(sections, share, feats), "pipe", 0, 0, tiled=True)
    mixed, xs = lax.optimization_barrier((mixed, xs))
    returned = lax.all_to_all(mixed, "tensor", 0, 0, tiled=True)

    expand = pl.pallas_call(
        expand_kernel,
        grid_spec=pltpu.PrefetchScalarGridSpec(
            num_scalar_prefetch=2,
            grid=(1,),
            in_specs=[
                pl.BlockSpec((1, pack_rows, feats), lambda i, s, t: (t[s[0]], 0, 0)),
                pl.BlockSpec((1, pack_rows, feats), lambda i, s, t: (t[s[0] - 1], 0, 0)),
                pl.BlockSpec((1, share, feats), lambda i, s, t: (s[0], 0, 0)),
            ],
            out_specs=[whole()] * 3,
        ),
        out_shape=[square, sds((pack_rows - LANES, feats), bf16), sds((2 * share, feats // 2), f32)],
        compiler_params=pltpu.CompilerParams(vmem_limit_bytes=EXPAND_MIB * 1024 * 1024),
        name="expand",
    )
    relay = pl.pallas_call(
        relay_kernel,
        in_specs=[whole()] * 5,
        out_specs=[whole()] * 2,
        out_shape=[value_shape, mixed_shape],
        scratch_shapes=[pltpu.VMEM((feats, feats), bf16)],
        compiler_params=pltpu.CompilerParams(vmem_limit_bytes=RELAY_MIB * 1024 * 1024),
        name="relay",
    )

    def prepare(s):
        return expand(jnp.full((1,), s, i32), table, packed, packed, xs)

    w1, w2, scale = prepare(sections - 1)
    stored = jnp.zeros((sections, share, feats), bf16)
    stored = lax.dynamic_update_index_in_dim(stored, g, sections - 1, 0)
    g, mixed = relay(returned, g, scale, w1, w2)

    def advance(k, carry):
        g, mixed, stored = carry
        s = sections - 2 - k
        returned = lax.all_to_all(mixed, "tensor", 0, 0, tiled=True)
        stored = lax.dynamic_update_index_in_dim(stored, g, s, 0)
        w1, w2, scale = prepare(s)
        g, mixed = relay(returned, g, scale, w1, w2)
        return (g, mixed, stored)

    g, _, stored = lax.fori_loop(0, sections - 2, advance, (g, mixed, stored))
    stored = lax.dynamic_update_index_in_dim(stored, g, 0, 0)
    stored, z = lax.optimization_barrier((stored, z))
    cotangent = lax.all_to_all(stored, "pipe", 0, 0, tiled=True)
    cotangent = cotangent.reshape(micros, tokens, feats)
    z, x_turned = pl.pallas_call(
        settle_kernel,
        grid=(micros,),
        in_specs=[payload_spec, token_spec, square_spec],
        out_specs=[feature_spec, feature_spec],
        out_shape=[sds((micros, feats, tokens), bf16)] * 2,
        compiler_params=params,
        name="settle",
    )(z, x, pick2)

    mixed = pl.pallas_call(
        owner_send_kernel,
        grid=(micros,),
        in_specs=[token_spec, square_spec],
        out_specs=payload_spec,
        out_shape=payload,
        compiler_params=params,
        name="owner_send",
    )(cotangent, w2d)
    returned = lax.all_to_all(mixed, "tensor", 0, 0, tiled=True)
    grads, first, second = pl.pallas_call(
        owner_kernel,
        grid=(micros,),
        in_specs=[
            whole(pltpu.SMEM),
            payload_spec,
            feature_spec,
            square_spec,
            weight_spec,
            feature_spec,
            feature_spec,
            token_spec,
        ],
        out_specs=[token_spec, weight_spec, weight_spec],
        out_shape=[sds(x.shape, bf16), sds((blocks, size, size), f32), sds((blocks, size, size), f32)],
        compiler_params=pltpu.CompilerParams(vmem_limit_bytes=OWNER_MIB * 1024 * 1024),
        name="owner",
    )(drop, returned, slope, pick1, w_first[0, 0], x_turned, z, cotangent)
    return (grads.reshape(section_inputs.shape), first[None, None], second[None, None])


def solution(mesh):
    placed = (
        P("pipe", None, None, "tensor"),
        P(None, None, "tensor"),
        P("pipe", None, "tensor", None, None),
        P("pipe", None, "tensor", None, None),
        P("pipe", None),
        P("pipe", None, None),
    )
    return jax.shard_map(
        on_device,
        mesh=mesh,
        in_specs=placed,
        out_specs=(
            P("pipe", None, None, "tensor"),
            P("pipe", None, "tensor", None, None),
            P("pipe", None, "tensor", None, None),
        ),
        check_vma=False,
    )
```

```python
import jax
import jax.numpy as jnp
from jax import lax
from jax.experimental import pallas as pl
from jax.experimental.pallas import tpu as pltpu
from jax.sharding import PartitionSpec as P

gelu_scale = 0.7978845608028654
gelu_cubic = 0.044715
bf16 = jnp.bfloat16
f32 = jnp.float32
i32 = jnp.int32
sds = jax.ShapeDtypeStruct

NN = ((1,), (0,))
NT = ((1,), (1,))
LANES = 128
IDS = 16
OWNER_MIB = 52
RELAY_MIB = 16
EXPAND_MIB = 16


def dot(left, right, dims):
    return lax.dot_general(left, right, (dims, ((), ())), preferred_element_type=f32)


def whole(space=pltpu.VMEM):
    return pl.BlockSpec(memory_space=space)


def gelu_pair(v):
    u = jnp.tanh(gelu_scale * (v + gelu_cubic * v * v * v))
    value = 0.5 * v * (1.0 + u)
    slope = 0.5 * (1.0 + u) + 0.5 * v * (1.0 - u * u) * gelu_scale * (1.0 + 3.0 * gelu_cubic * v * v)
    return value, slope


def prep_kernel(group_ref, drop_ref, perm_ref, w1_ref, w2_ref, packed_ref, w1d_ref, w2d_ref, pick1_ref, pick2_ref):
    feats = pick1_ref.shape[0]
    groups = perm_ref.shape[1] // feats
    blocks, size, _ = w1_ref.shape
    per_peer = feats // groups
    half = per_peer // 2
    own_group = group_ref[0]
    keep = drop_ref[0].astype(f32)
    base = own_group * feats
    rows = lax.broadcasted_iota(i32, (feats, feats), 0)
    cols = lax.broadcasted_iota(i32, (feats, feats), 1)
    before = jnp.where(rows < cols, 1.0, 0.0).astype(bf16)
    perm = jnp.concatenate([perm_ref[:, g * feats : (g + 1) * feats] for g in range(groups)], axis=0)
    mine = (perm >= base) & (perm < base + feats)
    rank = dot(jnp.where(mine, 1.0, 0.0).astype(bf16), before, NN)
    rank = jnp.where(mine, rank, -1.0).astype(i32)
    local = (perm - base).astype(f32)
    counter = lax.broadcasted_iota(i32, (half, feats), 0)
    lane = lax.broadcasted_iota(i32, (half, feats), 1)
    parts = []
    for part in range(2):
        for peer in range(groups):
            hit = counter + part * half == rank[peer : peer + 1, :]
            source = jnp.sum(jnp.where(hit, local[peer : peer + 1, :], 0.0), axis=1, keepdims=True)
            parts.append(jnp.where(lane == source.astype(i32), 1.0, 0.0))
    leave = jnp.concatenate(parts, axis=0).astype(bf16)
    start = lax.broadcasted_iota(i32, (groups, feats), 0)
    own = jnp.sum(jnp.where(start == own_group, perm, 0), axis=0, keepdims=True)
    from_group = (own >= start * feats) & (own < start * feats + feats)
    marks = jnp.where(from_group, 1.0, 0.0)
    place = dot(marks.astype(bf16), before, NN)
    place = place + jnp.where(place >= half, groups * half - half, 0.0) + start.astype(f32) * half
    slot = jnp.sum(marks * place, axis=0, keepdims=True).astype(i32)
    arrive = jnp.where(rows == slot, 1.0, 0.0)
    pick1_ref[...] = leave
    arrive_t = jnp.transpose(arrive).astype(bf16)
    pick2_ref[...] = arrive_t
    arrive = arrive.astype(bf16)
    part1 = jnp.zeros((size, feats), f32)
    part2 = jnp.zeros((size, feats), f32)
    for block in range(blocks):
        span = slice(block * size, (block + 1) * size)
        w1d_ref[:, span] = dot(leave[:, span], w1_ref[block], NT).astype(bf16)
        w2d_ref[:, span] = (keep * dot(arrive[:, span], w2_ref[block], NN)).astype(bf16)
        part1 += dot(w1_ref[block], leave[:, span], NT)
        part2 += keep * dot(jnp.transpose(w2_ref[block].astype(f32)).astype(bf16), arrive_t[span, :], NN)
    packed_ref[0:size, :] = part1.astype(bf16)
    packed_ref[size : 2 * size, :] = part2.astype(bf16)
    line = lax.broadcasted_iota(i32, (IDS, feats), 0)
    owner = (lax.broadcasted_iota(i32, (IDS, feats), 1) // size).astype(f32)
    ids = dot(jnp.where(line == 0, owner, 0.0).astype(bf16), leave, NT)
    ids += dot(jnp.where(line == 1, owner, 0.0).astype(bf16), arrive, NT)
    packed_ref[2 * size :, :] = ids.astype(bf16)


def to_payload(values, ref):
    groups, _, parts, half, tokens = ref.shape
    for part in range(parts):
        span = values[part * groups * half : (part + 1) * groups * half]
        ref[:, 0, part] = span.reshape(groups, half, tokens).astype(bf16)


def from_payload(ref):
    groups, _, parts, half, tokens = ref.shape
    return jnp.concatenate(
        [ref[:, 0, part].astype(f32).reshape(groups * half, tokens) for part in range(parts)], axis=0
    )


def forward_kernel(x_ref, w1d_ref, hidden_ref, slope_ref):
    value, slope = gelu_pair(dot(w1d_ref[...], x_ref[0], NT))
    to_payload(value, hidden_ref)
    slope_ref[0] = slope


def settle_kernel(z_ref, x_ref, pick2_ref, z_out, x_out):
    z_out[0] = dot(pick2_ref[...], from_payload(z_ref).astype(bf16), NN).astype(bf16)
    x_out[0] = jnp.transpose(x_ref[0].astype(f32)).astype(bf16)


def spread(values, ids, dense_ref):
    size = values.shape[0]
    for b in range(dense_ref.shape[0] // size):
        dense_ref[b * size : (b + 1) * size, :] = jnp.where(ids == b, values, 0.0).astype(bf16)


def expand_kernel(step_ref, table_ref, first_ref, second_ref, x_ref, w1_ref, w2_ref, slope_ref):
    del step_ref
    feats = x_ref.shape[2]
    first = first_ref[0].astype(f32)
    spread(first[:LANES], first[2 * LANES : 2 * LANES + 1], w1_ref)
    w2_ref[...] = second_ref[0, LANES:, :]
    v = dot(x_ref[0], w1_ref[...], NN)
    _, slope = gelu_pair(jnp.concatenate([v[:, : feats // 2], v[:, feats // 2 :]], axis=0))
    slope_ref[...] = slope


def mix(g, w2_ref, mixed_ref):
    feats = g.shape[1]
    s = dot(g, w2_ref[...], NN)
    s = jnp.concatenate([s[:, : feats // 2], s[:, feats // 2 :]], axis=0)
    mixed_ref[...] = jnp.transpose(s).reshape(mixed_ref.shape).astype(bf16)


def start_kernel(table_ref, g_ref, *refs):
    *place_refs, mixed_ref, packed_ref, w2_ref, sem = refs
    last = table_ref[table_ref.shape[0] - 1]
    for place, place_ref in enumerate(place_refs):

        @pl.when(last // 2 == place)
        def _():
            copy = pltpu.make_async_copy(place_ref.at[last % 2], packed_ref, sem)
            copy.start()
            copy.wait()

    packed = packed_ref[...].astype(f32)
    spread(packed[LANES : 2 * LANES], packed[2 * LANES + 1 : 2 * LANES + 2], w2_ref)
    mix(g_ref[...], w2_ref, mixed_ref)


def relay_kernel(returned_ref, g_in_ref, slope_ref, w1_ref, packed_ref, g_ref, mixed_ref, w2_ref):
    packed = packed_ref[...].astype(f32)
    spread(packed[:LANES], packed[LANES + 1 : LANES + 2], w2_ref)
    groups, half, lanes = returned_ref.shape
    tokens = lanes // 2
    dh = returned_ref[...].astype(f32).reshape(groups * half, lanes)
    da = (jnp.transpose(dh) * slope_ref[...]).astype(bf16)
    da = jnp.concatenate([da[:tokens], da[tokens:]], axis=1)
    g = (g_in_ref[...].astype(f32) + dot(da, w1_ref[...], NT)).astype(bf16)
    g_ref[...] = g
    mix(g, w2_ref, mixed_ref)


def owner_send_kernel(g_ref, w2d_ref, mixed_ref):
    to_payload(dot(w2d_ref[...], g_ref[0], NT), mixed_ref)


def owner_kernel(drop_ref, returned_ref, slope_ref, pick1_ref, w1_ref, x_ref, z_ref, g_ref, grads_ref, first_ref, second_ref):
    blocks, size, _ = first_ref.shape
    keep = drop_ref[0].astype(f32)
    da = jnp.transpose(from_payload(returned_ref) * slope_ref[0]).astype(bf16)
    da = dot(da, pick1_ref[...], NN).astype(bf16)

    @pl.when(pl.program_id(0) == 0)
    def _():
        first_ref[...] = jnp.zeros_like(first_ref)
        second_ref[...] = jnp.zeros_like(second_ref)

    for block in range(blocks):
        span = slice(block * size, (block + 1) * size)
        g = g_ref[0, :, span]
        grads_ref[0, :, span] = (g.astype(f32) + dot(da[:, span], w1_ref[block], NT)).astype(bf16)
        first_ref[block] += dot(x_ref[0, span, :], da[:, span], NN)
        second_ref[block] += keep * dot(z_ref[0, span, :], g, NN)


def on_device(section_inputs, out_grad, w_first, w_second, drop_flags, perm):
    sections = lax.axis_size("pipe")
    row = lax.axis_index("pipe").astype(i32)
    groups = lax.axis_size("tensor")
    group = lax.axis_index("tensor").astype(i32)
    feats = section_inputs.shape[3]
    tokens = 2 * section_inputs.shape[2]
    micros = section_inputs.shape[1] // 2
    x = section_inputs.reshape(micros, tokens, feats)
    share = micros * tokens // sections
    blocks, size = w_first.shape[2], w_first.shape[3]
    half = feats // groups // 2
    drop = drop_flags.reshape(1)
    params = pltpu.CompilerParams(vmem_limit_bytes=60 * 1024 * 1024)
    square = sds((feats, feats), bf16)
    pack_rows = 2 * LANES + IDS

    xs = lax.all_to_all(x.reshape(sections, share, feats), "pipe", 0, 0, tiled=True)

    packed, w1d, w2d, pick1, pick2 = pl.pallas_call(
        prep_kernel,
        in_specs=[whole(pltpu.SMEM), whole(pltpu.SMEM), whole(), whole(), whole()],
        out_specs=[whole()] * 5,
        out_shape=[sds((pack_rows, feats), bf16)] + [square] * 4,
        compiler_params=params,
        name="prep",
    )(group.reshape(1), drop, perm[0], w_first[0, 0], w_second[0, 0])
    chips = sections // 2
    core, chip = row % 2, row // 2
    swap = [(i, i ^ 1) for i in range(sections)]
    onward = [(2 * z, 2 * ((z + 1) % chips)) for z in range(chips)]
    onward += [(2 * z + 1, 2 * ((z - 1) % chips) + 1) for z in range(chips)]
    other = lax.ppermute(packed, "pipe", swap)
    current = jnp.stack([jnp.where(core == 0, packed, other), jnp.where(core == 0, other, packed)])
    places = [current] + [None] * (chips - 1)
    for distance in range(1, chips // 2 + 1):
        current = lax.ppermute(current, "pipe", onward)
        places[chips - distance] = current
        if 2 * distance < chips:
            places[distance] = lax.ppermute(current, "pipe", swap)
    packed = jnp.stack(places).reshape(sections, pack_rows, feats)
    index = jnp.arange(sections, dtype=i32)
    table = ((1 - 2 * core) * (index // 2 - chip)) % chips * 2 + index % 2

    payload = sds((groups, micros, 2, half, tokens), bf16)
    payload_spec = pl.BlockSpec((groups, 1, 2, half, tokens), lambda m: (0, m, 0, 0, 0))
    token_spec = pl.BlockSpec((1, tokens, feats), lambda m: (m, 0, 0))
    feature_spec = pl.BlockSpec((1, feats, tokens), lambda m: (m, 0, 0))
    square_spec = pl.BlockSpec((feats, feats), lambda m: (0, 0))
    weight_spec = pl.BlockSpec((blocks, size, size), lambda m: (0, 0, 0))

    hidden, slope = pl.pallas_call(
        forward_kernel,
        grid=(micros,),
        in_specs=[token_spec, square_spec],
        out_specs=[payload_spec, feature_spec],
        out_shape=[payload, sds((micros, feats, tokens), f32)],
        compiler_params=params,
        name="forward",
    )(x, w1d)
    mixed_shape = sds((groups, half, 2 * share), bf16)
    value_shape = sds((share, feats), bf16)
    g = lax.dynamic_index_in_dim(out_grad.reshape(sections, share, feats), row, 0, keepdims=False)
    mixed = pl.pallas_call(
        start_kernel,
        in_specs=[whole(pltpu.SMEM), whole()] + [whole(pl.ANY)] * chips,
        out_specs=whole(),
        out_shape=mixed_shape,
        scratch_shapes=[
            pltpu.VMEM((pack_rows, feats), bf16),
            pltpu.VMEM((feats, feats), bf16),
            pltpu.SemaphoreType.DMA,
        ],
        compiler_params=params,
        name="start",
    )(table, g, *places)
    hidden, xs = lax.optimization_barrier((hidden, xs))
    z = lax.all_to_all(hidden, "tensor", 0, 0, tiled=True)
    mixed, z = lax.optimization_barrier((mixed, z))
    returned = lax.all_to_all(mixed, "tensor", 0, 0, tiled=True)

    expand = pl.pallas_call(
        expand_kernel,
        grid_spec=pltpu.PrefetchScalarGridSpec(
            num_scalar_prefetch=2,
            grid=(1,),
            in_specs=[
                pl.BlockSpec((1, pack_rows, feats), lambda i, s, t: (t[s[0]], 0, 0)),
                pl.BlockSpec((1, pack_rows, feats), lambda i, s, t: (t[s[0] - 1], 0, 0)),
                pl.BlockSpec((1, share, feats), lambda i, s, t: (s[0], 0, 0)),
            ],
            out_specs=[whole()] * 3,
        ),
        out_shape=[square, sds((pack_rows - LANES, feats), bf16), sds((2 * share, feats // 2), f32)],
        compiler_params=pltpu.CompilerParams(vmem_limit_bytes=EXPAND_MIB * 1024 * 1024),
        name="expand",
    )
    relay = pl.pallas_call(
        relay_kernel,
        in_specs=[whole()] * 5,
        out_specs=[whole()] * 2,
        out_shape=[value_shape, mixed_shape],
        scratch_shapes=[pltpu.VMEM((feats, feats), bf16)],
        compiler_params=pltpu.CompilerParams(vmem_limit_bytes=RELAY_MIB * 1024 * 1024),
        name="relay",
    )

    def prepare(s):
        return expand(jnp.full((1,), s, i32), table, packed, packed, xs)

    w1, w2, scale = prepare(sections - 1)
    stored = jnp.zeros((sections, share, feats), bf16)
    stored = lax.dynamic_update_index_in_dim(stored, g, sections - 1, 0)
    g, mixed = relay(returned, g, scale, w1, w2)

    def advance(k, carry):
        g, mixed, stored = carry
        s = sections - 2 - k
        returned = lax.all_to_all(mixed, "tensor", 0, 0, tiled=True)
        stored = lax.dynamic_update_index_in_dim(stored, g, s, 0)
        w1, w2, scale = prepare(s)
        g, mixed = relay(returned, g, scale, w1, w2)
        return (g, mixed, stored)

    g, _, stored = lax.fori_loop(0, sections - 2, advance, (g, mixed, stored))
    stored = lax.dynamic_update_index_in_dim(stored, g, 0, 0)
    stored, z = lax.optimization_barrier((stored, z))
    cotangent = lax.all_to_all(stored, "pipe", 0, 0, tiled=True)
    cotangent = cotangent.reshape(micros, tokens, feats)
    z, x_turned = pl.pallas_call(
        settle_kernel,
        grid=(micros,),
        in_specs=[payload_spec, token_spec, square_spec],
        out_specs=[feature_spec, feature_spec],
        out_shape=[sds((micros, feats, tokens), bf16)] * 2,
        compiler_params=params,
        name="settle",
    )(z, x, pick2)

    mixed = pl.pallas_call(
        owner_send_kernel,
        grid=(micros,),
        in_specs=[token_spec, square_spec],
        out_specs=payload_spec,
        out_shape=payload,
        compiler_params=params,
        name="owner_send",
    )(cotangent, w2d)
    returned = lax.all_to_all(mixed, "tensor", 0, 0, tiled=True)
    grads, first, second = pl.pallas_call(
        owner_kernel,
        grid=(micros,),
        in_specs=[
            whole(pltpu.SMEM),
            payload_spec,
            feature_spec,
            square_spec,
            weight_spec,
            feature_spec,
            feature_spec,
            token_spec,
        ],
        out_specs=[token_spec, weight_spec, weight_spec],
        out_shape=[sds(x.shape, bf16), sds((blocks, size, size), f32), sds((blocks, size, size), f32)],
        compiler_params=pltpu.CompilerParams(vmem_limit_bytes=OWNER_MIB * 1024 * 1024),
        name="owner",
    )(drop, returned, slope, pick1, w_first[0, 0], x_turned, z, cotangent)
    return (grads.reshape(section_inputs.shape), first[None, None], second[None, None])


def solution(mesh):
    placed = (
        P("pipe", None, None, "tensor"),
        P(None, None, "tensor"),
        P("pipe", None, "tensor", None, None),
        P("pipe", None, "tensor", None, None),
        P("pipe", None),
        P("pipe", None, None),
    )
    return jax.shard_map(
        on_device,
        mesh=mesh,
        in_specs=placed,
        out_specs=(
            P("pipe", None, None, "tensor"),
            P("pipe", None, "tensor", None, None),
            P("pipe", None, "tensor", None, None),
        ),
        check_vma=False,
    )
```

```python
import jax
import jax.numpy as jnp
from jax import lax
from jax.experimental import pallas as pl
from jax.experimental.pallas import tpu as pltpu
from jax.sharding import PartitionSpec as P

gelu_scale = 0.7978845608028654
gelu_cubic = 0.044715
bf16 = jnp.bfloat16
f32 = jnp.float32
i32 = jnp.int32
sds = jax.ShapeDtypeStruct

NN = ((1,), (0,))
NT = ((1,), (1,))
LANES = 128
IDS = 16
OWNER_MIB = 52
RELAY_MIB = 16
EXPAND_MIB = 16


def dot(left, right, dims):
    return lax.dot_general(left, right, (dims, ((), ())), preferred_element_type=f32)


def whole(space=pltpu.VMEM):
    return pl.BlockSpec(memory_space=space)


def gelu_pair(v):
    u = jnp.tanh(gelu_scale * (v + gelu_cubic * v * v * v))
    value = 0.5 * v * (1.0 + u)
    slope = 0.5 * (1.0 + u) + 0.5 * v * (1.0 - u * u) * gelu_scale * (1.0 + 3.0 * gelu_cubic * v * v)
    return value, slope


def prep_kernel(group_ref, drop_ref, perm_ref, w1_ref, w2_ref, packed_ref, w1d_ref, w2d_ref, pick1_ref, pick2_ref):
    feats = pick1_ref.shape[0]
    groups = perm_ref.shape[1] // feats
    blocks, size, _ = w1_ref.shape
    per_peer = feats // groups
    half = per_peer // 2
    own_group = group_ref[0]
    keep = drop_ref[0].astype(f32)
    base = own_group * feats
    rows = lax.broadcasted_iota(i32, (feats, feats), 0)
    cols = lax.broadcasted_iota(i32, (feats, feats), 1)
    before = jnp.where(rows < cols, 1.0, 0.0).astype(bf16)
    perm = jnp.concatenate([perm_ref[:, g * feats : (g + 1) * feats] for g in range(groups)], axis=0)
    mine = (perm >= base) & (perm < base + feats)
    rank = dot(jnp.where(mine, 1.0, 0.0).astype(bf16), before, NN)
    rank = jnp.where(mine, rank, -1.0).astype(i32)
    local = (perm - base).astype(f32)
    counter = lax.broadcasted_iota(i32, (half, feats), 0)
    lane = lax.broadcasted_iota(i32, (half, feats), 1)
    parts = []
    for part in range(2):
        for peer in range(groups):
            hit = counter + part * half == rank[peer : peer + 1, :]
            source = jnp.sum(jnp.where(hit, local[peer : peer + 1, :], 0.0), axis=1, keepdims=True)
            parts.append(jnp.where(lane == source.astype(i32), 1.0, 0.0))
    leave = jnp.concatenate(parts, axis=0).astype(bf16)
    start = lax.broadcasted_iota(i32, (groups, feats), 0)
    own = jnp.sum(jnp.where(start == own_group, perm, 0), axis=0, keepdims=True)
    from_group = (own >= start * feats) & (own < start * feats + feats)
    marks = jnp.where(from_group, 1.0, 0.0)
    place = dot(marks.astype(bf16), before, NN)
    place = place + jnp.where(place >= half, groups * half - half, 0.0) + start.astype(f32) * half
    slot = jnp.sum(marks * place, axis=0, keepdims=True).astype(i32)
    arrive = jnp.where(rows == slot, 1.0, 0.0)
    pick1_ref[...] = leave
    arrive_t = jnp.transpose(arrive).astype(bf16)
    pick2_ref[...] = arrive_t
    arrive = arrive.astype(bf16)
    part1 = jnp.zeros((size, feats), f32)
    part2 = jnp.zeros((size, feats), f32)
    for block in range(blocks):
        span = slice(block * size, (block + 1) * size)
        w1d_ref[:, span] = dot(leave[:, span], w1_ref[block], NT).astype(bf16)
        w2d_ref[:, span] = (keep * dot(arrive[:, span], w2_ref[block], NN)).astype(bf16)
        part1 += dot(w1_ref[block], leave[:, span], NT)
        part2 += keep * dot(jnp.transpose(w2_ref[block].astype(f32)).astype(bf16), arrive_t[span, :], NN)
    packed_ref[0:size, :] = part1.astype(bf16)
    packed_ref[size : 2 * size, :] = part2.astype(bf16)
    line = lax.broadcasted_iota(i32, (IDS, feats), 0)
    owner = (lax.broadcasted_iota(i32, (IDS, feats), 1) // size).astype(f32)
    ids = dot(jnp.where(line == 0, owner, 0.0).astype(bf16), leave, NT)
    ids += dot(jnp.where(line == 1, owner, 0.0).astype(bf16), arrive, NT)
    packed_ref[2 * size :, :] = ids.astype(bf16)


def to_payload(values, ref):
    groups, _, parts, half, tokens = ref.shape
    for part in range(parts):
        span = values[part * groups * half : (part + 1) * groups * half]
        ref[:, 0, part] = span.reshape(groups, half, tokens).astype(bf16)


def from_payload(ref):
    groups, _, parts, half, tokens = ref.shape
    return jnp.concatenate(
        [ref[:, 0, part].astype(f32).reshape(groups * half, tokens) for part in range(parts)], axis=0
    )


def forward_kernel(x_ref, w1d_ref, hidden_ref, slope_ref):
    value, slope = gelu_pair(dot(w1d_ref[...], x_ref[0], NT))
    to_payload(value, hidden_ref)
    slope_ref[0] = slope


def settle_kernel(z_ref, x_ref, pick2_ref, z_out, x_out):
    z_out[0] = dot(pick2_ref[...], from_payload(z_ref).astype(bf16), NN).astype(bf16)
    x_out[0] = jnp.transpose(x_ref[0].astype(f32)).astype(bf16)


def spread(values, ids, dense_ref):
    size = values.shape[0]
    for b in range(dense_ref.shape[0] // size):
        dense_ref[b * size : (b + 1) * size, :] = jnp.where(ids == b, values, 0.0).astype(bf16)


def expand_kernel(step_ref, table_ref, first_ref, second_ref, x_ref, w1_ref, w2_ref, slope_ref):
    del step_ref
    feats = x_ref.shape[2]
    first = first_ref[0].astype(f32)
    spread(first[:LANES], first[2 * LANES : 2 * LANES + 1], w1_ref)
    w2_ref[...] = second_ref[0, LANES:, :]
    v = dot(x_ref[0], w1_ref[...], NN)
    _, slope = gelu_pair(jnp.concatenate([v[:, : feats // 2], v[:, feats // 2 :]], axis=0))
    slope_ref[...] = slope


def mix(g, w2_ref, mixed_ref):
    feats = g.shape[1]
    s = dot(g, w2_ref[...], NN)
    s = jnp.concatenate([s[:, : feats // 2], s[:, feats // 2 :]], axis=0)
    mixed_ref[...] = jnp.transpose(s).reshape(mixed_ref.shape).astype(bf16)


def start_kernel(table_ref, g_ref, *refs):
    *place_refs, mixed_ref, packed_ref, w2_ref, sem = refs
    last = table_ref[table_ref.shape[0] - 1]
    for place, place_ref in enumerate(place_refs):

        @pl.when(last == place)
        def _():
            copy = pltpu.make_async_copy(place_ref, packed_ref, sem)
            copy.start()
            copy.wait()

    packed = packed_ref[...].astype(f32)
    spread(packed[LANES : 2 * LANES], packed[2 * LANES + 1 : 2 * LANES + 2], w2_ref)
    mix(g_ref[...], w2_ref, mixed_ref)


def relay_kernel(returned_ref, g_in_ref, slope_ref, w1_ref, packed_ref, g_ref, mixed_ref, w2_ref):
    packed = packed_ref[...].astype(f32)
    spread(packed[:LANES], packed[LANES + 1 : LANES + 2], w2_ref)
    groups, half, lanes = returned_ref.shape
    tokens = lanes // 2
    dh = returned_ref[...].astype(f32).reshape(groups * half, lanes)
    da = (jnp.transpose(dh) * slope_ref[...]).astype(bf16)
    da = jnp.concatenate([da[:tokens], da[tokens:]], axis=1)
    g = (g_in_ref[...].astype(f32) + dot(da, w1_ref[...], NT)).astype(bf16)
    g_ref[...] = g
    mix(g, w2_ref, mixed_ref)


def owner_send_kernel(g_ref, w2d_ref, mixed_ref):
    to_payload(dot(w2d_ref[...], g_ref[0], NT), mixed_ref)


def owner_kernel(drop_ref, returned_ref, slope_ref, pick1_ref, w1_ref, x_ref, z_ref, g_ref, grads_ref, first_ref, second_ref):
    blocks, size, _ = first_ref.shape
    keep = drop_ref[0].astype(f32)
    da = jnp.transpose(from_payload(returned_ref) * slope_ref[0]).astype(bf16)
    da = dot(da, pick1_ref[...], NN).astype(bf16)

    @pl.when(pl.program_id(0) == 0)
    def _():
        first_ref[...] = jnp.zeros_like(first_ref)
        second_ref[...] = jnp.zeros_like(second_ref)

    for block in range(blocks):
        span = slice(block * size, (block + 1) * size)
        g = g_ref[0, :, span]
        grads_ref[0, :, span] = (g.astype(f32) + dot(da[:, span], w1_ref[block], NT)).astype(bf16)
        first_ref[block] += dot(x_ref[0, span, :], da[:, span], NN)
        second_ref[block] += keep * dot(z_ref[0, span, :], g, NN)


def on_device(section_inputs, out_grad, w_first, w_second, drop_flags, perm):
    sections = lax.axis_size("pipe")
    row = lax.axis_index("pipe").astype(i32)
    groups = lax.axis_size("tensor")
    group = lax.axis_index("tensor").astype(i32)
    feats = section_inputs.shape[3]
    tokens = 2 * section_inputs.shape[2]
    micros = section_inputs.shape[1] // 2
    x = section_inputs.reshape(micros, tokens, feats)
    share = micros * tokens // sections
    blocks, size = w_first.shape[2], w_first.shape[3]
    half = feats // groups // 2
    drop = drop_flags.reshape(1)
    params = pltpu.CompilerParams(vmem_limit_bytes=60 * 1024 * 1024)
    square = sds((feats, feats), bf16)
    pack_rows = 2 * LANES + IDS

    packed, w1d, w2d, pick1, pick2 = pl.pallas_call(
        prep_kernel,
        in_specs=[whole(pltpu.SMEM), whole(pltpu.SMEM), whole(), whole(), whole()],
        out_specs=[whole()] * 5,
        out_shape=[sds((pack_rows, feats), bf16)] + [square] * 4,
        compiler_params=params,
        name="prep",
    )(group.reshape(1), drop, perm[0], w_first[0, 0], w_second[0, 0])
    chips = sections // 2
    core, chip = row % 2, row // 2
    swap = [(i, i ^ 1) for i in range(sections)]
    onward = [(2 * z, 2 * ((z + 1) % chips)) for z in range(chips)]
    onward += [(2 * z + 1, 2 * ((z - 1) % chips) + 1) for z in range(chips)]
    other = lax.ppermute(packed, "pipe", swap)
    places = [None] * sections
    for which in range(2):
        current = jnp.where(core == which, packed, other)
        places[which] = current
        for distance in range(1, chips // 2 + 1):
            current = lax.ppermute(current, "pipe", onward)
            places[2 * (chips - distance) + which] = current
            if 2 * distance < chips:
                places[2 * distance + which] = lax.ppermute(current, "pipe", swap)
    index = jnp.arange(sections, dtype=i32)
    table = ((1 - 2 * core) * (index // 2 - chip)) % chips * 2 + index % 2

    payload = sds((groups, micros, 2, half, tokens), bf16)
    payload_spec = pl.BlockSpec((groups, 1, 2, half, tokens), lambda m: (0, m, 0, 0, 0))
    token_spec = pl.BlockSpec((1, tokens, feats), lambda m: (m, 0, 0))
    feature_spec = pl.BlockSpec((1, feats, tokens), lambda m: (m, 0, 0))
    square_spec = pl.BlockSpec((feats, feats), lambda m: (0, 0))
    weight_spec = pl.BlockSpec((blocks, size, size), lambda m: (0, 0, 0))

    hidden, slope = pl.pallas_call(
        forward_kernel,
        grid=(micros,),
        in_specs=[token_spec, square_spec],
        out_specs=[payload_spec, feature_spec],
        out_shape=[payload, sds((micros, feats, tokens), f32)],
        compiler_params=params,
        name="forward",
    )(x, w1d)
    mixed_shape = sds((groups, half, 2 * share), bf16)
    value_shape = sds((share, feats), bf16)
    g = lax.dynamic_index_in_dim(out_grad.reshape(sections, share, feats), row, 0, keepdims=False)
    z = lax.all_to_all(hidden, "tensor", 0, 0, tiled=True)
    to_share, z, places = lax.optimization_barrier((x, z, places))
    xs = lax.all_to_all(to_share.reshape(sections, share, feats), "pipe", 0, 0, tiled=True)
    packed = jnp.stack(places)
    mixed = pl.pallas_call(
        start_kernel,
        in_specs=[whole(pltpu.SMEM), whole()] + [whole(pl.ANY)] * sections,
        out_specs=whole(),
        out_shape=mixed_shape,
        scratch_shapes=[
            pltpu.VMEM((pack_rows, feats), bf16),
            pltpu.VMEM((feats, feats), bf16),
            pltpu.SemaphoreType.DMA,
        ],
        compiler_params=params,
        name="start",
    )(table, g, *places)
    mixed, xs = lax.optimization_barrier((mixed, xs))
    returned = lax.all_to_all(mixed, "tensor", 0, 0, tiled=True)

    expand = pl.pallas_call(
        expand_kernel,
        grid_spec=pltpu.PrefetchScalarGridSpec(
            num_scalar_prefetch=2,
            grid=(1,),
            in_specs=[
                pl.BlockSpec((1, pack_rows, feats), lambda i, s, t: (t[s[0]], 0, 0)),
                pl.BlockSpec((1, pack_rows, feats), lambda i, s, t: (t[s[0] - 1], 0, 0)),
                pl.BlockSpec((1, share, feats), lambda i, s, t: (s[0], 0, 0)),
            ],
            out_specs=[whole()] * 3,
        ),
        out_shape=[square, sds((pack_rows - LANES, feats), bf16), sds((2 * share, feats // 2), f32)],
        compiler_params=pltpu.CompilerParams(vmem_limit_bytes=EXPAND_MIB * 1024 * 1024),
        name="expand",
    )
    relay = pl.pallas_call(
        relay_kernel,
        in_specs=[whole()] * 5,
        out_specs=[whole()] * 2,
        out_shape=[value_shape, mixed_shape],
        scratch_shapes=[pltpu.VMEM((feats, feats), bf16)],
        compiler_params=pltpu.CompilerParams(vmem_limit_bytes=RELAY_MIB * 1024 * 1024),
        name="relay",
    )

    def prepare(s):
        return expand(jnp.full((1,), s, i32), table, packed, packed, xs)

    w1, w2, scale = prepare(sections - 1)
    stored = jnp.zeros((sections, share, feats), bf16)
    stored = lax.dynamic_update_index_in_dim(stored, g, sections - 1, 0)
    g, mixed = relay(returned, g, scale, w1, w2)

    def advance(k, carry):
        g, mixed, stored = carry
        s = sections - 2 - k
        returned = lax.all_to_all(mixed, "tensor", 0, 0, tiled=True)
        stored = lax.dynamic_update_index_in_dim(stored, g, s, 0)
        w1, w2, scale = prepare(s)
        g, mixed = relay(returned, g, scale, w1, w2)
        return (g, mixed, stored)

    g, _, stored = lax.fori_loop(0, sections - 2, advance, (g, mixed, stored))
    stored = lax.dynamic_update_index_in_dim(stored, g, 0, 0)
    stored, z = lax.optimization_barrier((stored, z))
    cotangent = lax.all_to_all(stored, "pipe", 0, 0, tiled=True)
    cotangent = cotangent.reshape(micros, tokens, feats)
    z, x_turned = pl.pallas_call(
        settle_kernel,
        grid=(micros,),
        in_specs=[payload_spec, token_spec, square_spec],
        out_specs=[feature_spec, feature_spec],
        out_shape=[sds((micros, feats, tokens), bf16)] * 2,
        compiler_params=params,
        name="settle",
    )(z, x, pick2)

    mixed = pl.pallas_call(
        owner_send_kernel,
        grid=(micros,),
        in_specs=[token_spec, square_spec],
        out_specs=payload_spec,
        out_shape=payload,
        compiler_params=params,
        name="owner_send",
    )(cotangent, w2d)
    returned = lax.all_to_all(mixed, "tensor", 0, 0, tiled=True)
    grads, first, second = pl.pallas_call(
        owner_kernel,
        grid=(micros,),
        in_specs=[
            whole(pltpu.SMEM),
            payload_spec,
            feature_spec,
            square_spec,
            weight_spec,
            feature_spec,
            feature_spec,
            token_spec,
        ],
        out_specs=[token_spec, weight_spec, weight_spec],
        out_shape=[sds(x.shape, bf16), sds((blocks, size, size), f32), sds((blocks, size, size), f32)],
        compiler_params=pltpu.CompilerParams(vmem_limit_bytes=OWNER_MIB * 1024 * 1024),
        name="owner",
    )(drop, returned, slope, pick1, w_first[0, 0], x_turned, z, cotangent)
    return (grads.reshape(section_inputs.shape), first[None, None], second[None, None])


def solution(mesh):
    placed = (
        P("pipe", None, None, "tensor"),
        P(None, None, "tensor"),
        P("pipe", None, "tensor", None, None),
        P("pipe", None, "tensor", None, None),
        P("pipe", None),
        P("pipe", None, None),
    )
    return jax.shard_map(
        on_device,
        mesh=mesh,
        in_specs=placed,
        out_specs=(
            P("pipe", None, None, "tensor"),
            P("pipe", None, "tensor", None, None),
            P("pipe", None, "tensor", None, None),
        ),
        check_vma=False,
    )
```
